128 devices in a mesh: dp: 16 (over z, y_hi, core), tensor: 8 (over x, y_lo).
Axes of the slice: x: 4, y: 4 (y_hi: 2, y_lo: 2; y = y_hi * 2 + y_lo), z: 4, core: 2. Of those that a mesh axis runs over, the one named last changes fastest.
Arguments:
- history: bfloat16 [4, 3072, 4096], P(None, 'dp'), may hold values from -6 to 6
- depth_weights: float32 [4], replicated, may hold values from 0.2 to 1
- depth_index: int32 [4], replicated, may hold values from 0 to 3
- gain: float32 [4096], replicated, may hold values from 0.1 to 1.9
- gate_blocks: bfloat16 [896, 128, 128], P(('tensor', 'dp')), may hold values from -0.1875 to 0.1875
- up_blocks: bfloat16 [896, 128, 128], P(('tensor', 'dp')), may hold values from -0.1875 to 0.1875
- down_blocks: bfloat16 [896, 128, 128], P(('tensor', 'dp')), may hold values from -0.09375 to 0.09375
- block_ids: int32 [896, 2], P('tensor'), may hold values from 0 to 31, as said below
- grad_out: bfloat16 [3072, 4096], P('dp'), may hold values from -16 to 16
Outputs:
- layer_out: bfloat16 [3072, 4096], P('dp', 'tensor')
- grad_mixed: float32 [3072, 4096], P('dp', 'tensor')
- grad_gate: float32 [896, 128, 128], P(('tensor', 'dp'))
- grad_up: float32 [896, 128, 128], P(('tensor', 'dp'))
- grad_down: float32 [896, 128, 128], P(('tensor', 'dp'))
- grad_depth: float32 [4], replicated
- grad_gain: float32 [4096], P('tensor')
The draws below stay inside these ranges and needn't reach their ends.
Inputs may be any that keep to these rules, and one draw needn't show every extreme that they name: `block_ids`: within the 112 rows of one index of tensor the pairs are distinct; column 0 is a row block below 32, column 1 a column block below 14 counted within that index's hidden units.
All inputs are finite; a program needn't handle non-finite values.
Results may differ from the reference program's by a relative error of at most 0.025.
Values may be sent and summed in bfloat16 or wider, within the bound.
No kernel may reach another device: no remote copies, remote signals or barrier semaphores. Data moves between devices by JAX's collectives and lax.ppermute only.
A program may use at most 192 MiB of HBM per device.

```python
import jax
import jax.numpy as jnp
from jax import lax

D = 4096
FF = 14336
BS = 128
HIST = 4
NW = 4
TOK_DEV = 192
TOKENS = 3072
RB = 32
HB = 14
NBLK_SH = 112
NBLK = 896
N_DP = 16
N_TENSOR = 8


def draw_block_ids(key, part):
    shards = NBLK // NBLK_SH
    subkeys = jax.random.split(key, shards)

    def choose_shard(subkey):
        return jax.random.permutation(subkey, RB * HB)[:NBLK_SH]
    chosen = jax.vmap(choose_shard)(subkeys).reshape(NBLK).astype(jnp.int32)
    return jnp.stack([chosen // HB, chosen % HB], axis=1).astype(jnp.int32)


def draw_grad_out(key, part):
    position = jnp.arange(TOKENS, dtype=jnp.float32) / (TOKENS - 1)
    values = jnp.clip(jax.random.normal(key, (TOKENS, D), jnp.float32), -4.0, 4.0)
    values = values * (1.0 + 2.0 * position)[:, None]
    return values.astype(jnp.bfloat16)


def plant(result, own_key, low, top_value):
    longest = result.shape.index(max(result.shape))
    spots = []
    for shift in (0, 1):
        where = [jax.random.randint(jax.random.fold_in(own_key, axis), (), 0, length) for axis, length in enumerate(result.shape)]
        where[longest] = (where[longest] + shift) % result.shape[longest]
        spots.append(tuple(where))
    return result.at[spots[0]].set(low).at[spots[1]].set(top_value)


def shard_levels(own_key, shape, cuts, low, top_value):
    factor_of, own = 1.0, jax.random.fold_in(own_key, 6)
    for dim, shards_of in cuts:
        draws = jnp.exp(jax.random.uniform(jax.random.fold_in(own, dim), (shards_of,), jnp.float32, low / len(cuts), top_value / len(cuts)))
        factor_of = factor_of * jnp.repeat(draws, shape[dim] // shards_of).reshape([-1 if axis == dim else 1 for axis in range(len(shape))])
    return factor_of


def scatter_about(rng, extent, deviation, limit, cuts=(), held_as=jnp.bfloat16):
    factor_of = shard_levels(rng, extent, cuts, -0.22, 0.18) if cuts else 1.0
    values = jax.random.normal(rng, extent, jnp.float32) * deviation * factor_of
    return jnp.minimum(jnp.maximum(values, -limit), limit).astype(held_as)


def setup_inputs(seed: int = 0) -> dict:
    splits = jax.random.split(jax.random.key(seed), 10)
    history = scatter_about(splits[0], (HIST, TOKENS, D), 1.0, 6.0, ((1, 16),))
    depth_weights = jnp.clip(jax.random.uniform(splits[1], (NW,), jnp.float32, 0.2, 1.0), 0.2, 1.0)
    depth_index = plant(jax.random.randint(splits[2], (NW,), 0, HIST), jax.random.fold_in(splits[2], 1), 0, HIST - 1).astype(jnp.int32)
    gain = jnp.clip(1.0 + 0.18 * jax.random.normal(splits[3], (D,), jnp.float32), 0.1, 1.9)
    gate_blocks = scatter_about(splits[4], (NBLK, BS, BS), (D // 4) ** -0.5, 0.1875, ((0, 128),))
    up_blocks = scatter_about(splits[5], (NBLK, BS, BS), (D // 4) ** -0.5, 0.1875, ((0, 128),))
    down_blocks = scatter_about(splits[6], (NBLK, BS, BS), (FF // 4) ** -0.5, 0.09375, ((0, 128),))
    block_ids = draw_block_ids(jax.random.fold_in(splits[9], 71), 0)
    grad_out = draw_grad_out(jax.random.fold_in(splits[9], 71), 0)
    return dict(history=history, depth_weights=depth_weights, depth_index=depth_index, gain=gain, gate_blocks=gate_blocks, up_blocks=up_blocks, down_blocks=down_blocks, block_ids=block_ids, grad_out=grad_out)


EPSILON = 1e-05

def norm_rows(mixed, gain):
    scale_inv = lax.rsqrt(lax.optimization_barrier(jnp.mean(mixed * mixed, axis=-1, keepdims=True)) + EPSILON)
    return mixed * scale_inv * gain

def group_sum(left_rows, right_rows):
    left_groups = left_rows.astype(jnp.float32).reshape(N_DP, TOK_DEV, -1, BS)
    right_groups = right_rows.astype(jnp.float32).reshape(N_DP, TOK_DEV, -1, BS)
    partial_terms = jnp.einsum('gtbi,gtbj->gbij', left_groups, right_groups)
    rounded = lax.optimization_barrier(partial_terms.astype(jnp.bfloat16))
    return lax.optimization_barrier(jnp.sum(rounded.astype(jnp.float32), axis=0))

def reference(history, depth_weights, depth_index, gain, gate_blocks, up_blocks, down_blocks, block_ids, grad_out):
    mixed = jnp.zeros((TOKENS, D), jnp.float32)
    for layer_slot in range(NW):
        earlier = lax.dynamic_index_in_dim(history, depth_index[layer_slot], 0, keepdims=False)
        mixed = mixed + depth_weights[layer_slot] * earlier.astype(jnp.float32)
    normed = norm_rows(mixed, gain).astype(jnp.bfloat16)
    normed3 = normed.reshape(TOKENS, RB, BS)
    out3 = grad_out.reshape(TOKENS, RB, BS)
    shard_pairs = block_ids.reshape(N_TENSOR, NBLK_SH, 2)
    gate_shards = gate_blocks.reshape(N_TENSOR, NBLK_SH, BS, BS)
    up_shards = up_blocks.reshape(N_TENSOR, NBLK_SH, BS, BS)
    down_shards = down_blocks.reshape(N_TENSOR, NBLK_SH, BS, BS)

    def hidden_parts(row_ids, col_ids, gate_w, up_w):
        picked = jnp.take(normed3, row_ids, axis=1).astype(jnp.float32)
        zero_cols = jnp.zeros((TOKENS, HB, BS), jnp.float32)
        gate = zero_cols.at[:, col_ids].add(jnp.einsum('tbi,bij->tbj', picked, gate_w.astype(jnp.float32)))
        up = zero_cols.at[:, col_ids].add(jnp.einsum('tbi,bij->tbj', picked, up_w.astype(jnp.float32)))
        hidden = (jax.nn.silu(gate) * up).astype(jnp.bfloat16)
        return (gate, up, hidden)

    def forward_step(totals, shard_data):
        block_pairs, gate_w, up_w, down_w = shard_data
        row_ids = block_pairs[:, 0]
        col_ids = block_pairs[:, 1]
        gate, up, hidden = hidden_parts(row_ids, col_ids, gate_w, up_w)
        picked = jnp.take(hidden, col_ids, axis=1).astype(jnp.float32)
        totals = totals.at[:, row_ids].add(jnp.einsum('tbi,bij->tbj', picked, down_w.astype(jnp.float32)))
        return (totals, None)
    zero_rows = jnp.zeros((TOKENS, RB, BS), jnp.float32)
    ffn3, unused = lax.scan(forward_step, zero_rows, (shard_pairs, gate_shards, up_shards, down_shards))
    layer_out = (mixed + ffn3.reshape(TOKENS, D)).astype(jnp.bfloat16)

    def backward_step(totals, shard_data):
        block_pairs, gate_w, up_w, down_w = shard_data
        row_ids = block_pairs[:, 0]
        col_ids = block_pairs[:, 1]
        gate, up, hidden = hidden_parts(row_ids, col_ids, gate_w, up_w)
        out_rows = jnp.take(out3, row_ids, axis=1)
        zero_cols = jnp.zeros((TOKENS, HB, BS), jnp.float32)
        grad_hidden = zero_cols.at[:, col_ids].add(jnp.einsum('tbj,bij->tbi', out_rows.astype(jnp.float32), down_w.astype(jnp.float32)))
        sigmoid_gate = jax.nn.sigmoid(gate)
        grad_gate_pre = (grad_hidden * up * sigmoid_gate * (1.0 + gate * (1.0 - sigmoid_gate))).astype(jnp.bfloat16)
        grad_up_pre = (grad_hidden * gate * sigmoid_gate).astype(jnp.bfloat16)
        gate_cols = jnp.take(grad_gate_pre, col_ids, axis=1)
        up_cols = jnp.take(grad_up_pre, col_ids, axis=1)
        contrib = jnp.einsum('tbj,bij->tbi', gate_cols.astype(jnp.float32), gate_w.astype(jnp.float32))
        contrib = contrib + jnp.einsum('tbj,bij->tbi', up_cols.astype(jnp.float32), up_w.astype(jnp.float32))
        totals = totals.at[:, row_ids].add(contrib)
        in_rows = jnp.take(normed3, row_ids, axis=1)
        hidden_cols = jnp.take(hidden, col_ids, axis=1)
        block_grads = jnp.stack([group_sum(in_rows, gate_cols), group_sum(in_rows, up_cols), group_sum(hidden_cols, out_rows)], axis=1)
        return (totals, block_grads)
    grad_normed3, block_grads = lax.scan(backward_step, zero_rows, (shard_pairs, gate_shards, up_shards, down_shards))
    block_grads = block_grads.reshape(NBLK, 3, BS, BS)
    grad_normed = grad_normed3.reshape(TOKENS, D)
    ignored, pull_back = jax.vjp(norm_rows, mixed, gain)
    grad_x, grad_gain = pull_back(grad_normed)
    grad_mixed = grad_out.astype(jnp.float32) + grad_x
    depth_list = []
    for layer_slot in range(NW):
        earlier = lax.dynamic_index_in_dim(history, depth_index[layer_slot], 0, keepdims=False)
        depth_list.append(jnp.sum(grad_mixed * earlier.astype(jnp.float32)))
    grad_depth = jnp.stack(depth_list)
    return (layer_out, grad_mixed, block_grads[:, 0], block_grads[:, 1], block_grads[:, 2], grad_depth, grad_gain)
```

```python
import functools

import jax
import jax.numpy as jnp
from jax import lax
from jax.experimental import pallas as pl
from jax.experimental.pallas import tpu as pltpu
from jax.sharding import PartitionSpec as P

EPSILON = 1e-05
BS = 128
N_Z, N_Y, N_CORE = 4, 2, 2
N_X, N_YLO = 4, 2
N_DP = N_Z * N_Y * N_CORE
N_TENSOR = N_X * N_YLO
CHIPS = N_Z * N_Y
OWN, YY, A1, B1, A2, YA, YB, Y2 = range(8)
EXTRA = 16
TILE = 16
VMEM_LIMIT = 60 * 1024 * 1024


BF = jnp.bfloat16
F32 = jnp.float32


def sign_of(core):
    return 1 - 2 * core


def dp_perm(kind):
    pairs = []
    for z in range(N_Z):
        for y in range(N_Y):
            for core in range(N_CORE):
                tz, ty, tc = z, y, core
                if kind == "a":
                    tz = (z + sign_of(core)) % N_Z
                elif kind == "b":
                    tz = (z - sign_of(core)) % N_Z
                elif kind == "y":
                    ty = 1 - y
                elif kind == "c":
                    tc = 1 - core
                elif kind == "z1":
                    tz = z ^ 1
                elif kind == "z2":
                    tz = z ^ 2
                pairs.append(((z * N_Y + y) * N_CORE + core, (tz * N_Y + ty) * N_CORE + tc))
    return pairs


def tensor_perm(kind):
    pairs = []
    for dp in range(N_DP):
        step = sign_of(dp % N_CORE)
        for x in range(N_X):
            for ylo in range(N_YLO):
                tx, ty = x, ylo
                if kind == "a":
                    tx = (x + step) % N_X
                elif kind == "b":
                    tx = (x - step) % N_X
                else:
                    ty = 1 - ylo
                pairs.append((dp * N_TENSOR + x * N_YLO + ylo, dp * N_TENSOR + tx * N_YLO + ty))
    return pairs


def over_dp(value, kind):
    return lax.ppermute(value, "dp", dp_perm(kind))


def over_tensor(value, kind):
    return lax.ppermute(value, ("dp", "tensor"), tensor_perm(kind))


def spec(space):
    return pl.BlockSpec(memory_space=space)


def lanes(index, size=BS):
    return pl.ds(pl.multiple_of(index * size, size), size)


def mm(left, right):
    return jnp.dot(left, right, preferred_element_type=F32)


def mm_t(left, right):
    return lax.dot_general(left, right, (((1,), (1,)), ((), ())), preferred_element_type=F32)


def mm_l(left, right):
    return lax.dot_general(left, right, (((0,), (0,)), ((), ())), preferred_element_type=F32)


def norm_kernel(index, weights, h0, h1, h2, h3, grad_out, gain, normed, stats):
    layers = [h[0].astype(F32) for h in (h0, h1, h2, h3)]
    width = layers[0].shape[1]
    mixed = weights[0] * layers[0]
    for slot in range(1, 4):
        mixed = mixed + weights[slot] * layers[slot]
    scale = lax.rsqrt(jnp.sum(mixed * mixed, axis=-1, keepdims=True) / width + EPSILON)
    normed[...] = (mixed * scale * gain[...]).astype(BF)
    cot = grad_out[...].astype(F32)
    lane = lax.broadcasted_iota(jnp.int32, stats.shape, 1)
    found = jnp.where(lane == 0, scale, 0.0)
    for slot in range(4):
        found = jnp.where(lane == 1 + slot, jnp.sum(mixed * layers[slot], axis=-1, keepdims=True), found)
        found = jnp.where(lane == 5 + slot, jnp.sum(cot * layers[slot], axis=-1, keepdims=True), found)
    stats[...] = found


def norm_call(depth_index, depth_weights, history, grad_out, gain):
    tokens, width = grad_out.shape

    def layer_spec(slot):
        return pl.BlockSpec((1, TILE, width), lambda i, index: (index[slot], i, 0))

    return pl.pallas_call(
        norm_kernel,
        out_shape=(
            jax.ShapeDtypeStruct((tokens, width), BF),
            jax.ShapeDtypeStruct((tokens, BS), F32),
        ),
        grid_spec=pltpu.PrefetchScalarGridSpec(
            num_scalar_prefetch=1,
            grid=(tokens // TILE,),
            in_specs=[spec(pltpu.SMEM)]
            + [layer_spec(slot) for slot in range(4)]
            + [
                pl.BlockSpec((TILE, width), lambda i, index: (i, 0)),
                pl.BlockSpec((1, width), lambda i, index: (0, 0)),
            ],
            out_specs=[
                pl.BlockSpec((TILE, width), lambda i, index: (i, 0)),
                pl.BlockSpec((TILE, BS), lambda i, index: (i, 0)),
            ],
        ),
        compiler_params=pltpu.CompilerParams(vmem_limit_bytes=VMEM_LIMIT),
        cost_estimate=pl.CostEstimate(flops=tokens * width * 30, bytes_accessed=tokens * width * 12, transcendentals=0),
        name="norm",
    )(depth_index, depth_weights, history, history, history, history, grad_out, gain.reshape(1, width))


def load_pair(shards, buffer, sems, share):
    copies = []
    for slot, shard in enumerate(shards):
        for part in range(2):
            copies.append(
                pltpu.make_async_copy(
                    shard.at[pl.ds(part * share, share)],
                    buffer.at[pl.ds(slot * share, share), :, pl.ds(part * BS, BS)],
                    sems.at[slot, part],
                )
            )
    return copies


def load_single(shards, buffer, sems, share):
    return [
        pltpu.make_async_copy(shard, buffer.at[pl.ds(slot * share, share)], sems.at[slot])
        for slot, shard in enumerate(shards)
    ]


def forward_kernel(share, *refs):
    order, rows, cols, normed, grad_out = refs[:5]
    shards = refs[5 : 5 + N_DP]
    gate_up, hidden, mine, other = refs[5 + N_DP : 9 + N_DP]
    held, down_grads, load_sems, store_sems = refs[9 + N_DP :]
    copies = load_pair(shards, held, load_sems, share)
    for copy in copies:
        copy.start()
    gate_up[...] = jnp.zeros_like(gate_up)
    for copy in copies:
        copy.wait()

    def project(slot, carry):
        base = order[slot] * share
        for j in range(share):
            row, col = rows[base + j], cols[base + j]
            gate_up[col] += mm(normed[:, lanes(row)], held[slot * share + j])
        return carry

    lax.fori_loop(0, N_DP, project, 0)

    def activate(col, carry):
        gate = gate_up[col, :, 0:BS]
        up = gate_up[col, :, BS:]
        hidden[col] = (gate / (1.0 + jnp.exp(-gate)) * up).astype(BF)
        return carry

    lax.fori_loop(0, hidden.shape[0], activate, 0)

    def down_grad(slot, carry):
        base = order[slot] * share
        for j in range(share):
            row, col = rows[base + j], cols[base + j]
            down_grads[slot, j] = mm_l(hidden[col], grad_out[:, lanes(row)]).astype(BF)
        return carry

    lax.fori_loop(0, N_DP, down_grad, 0)
    stores = [
        pltpu.make_async_copy(
            down_grads.at[slot],
            (mine if slot < CHIPS else other).at[slot % CHIPS, pl.ds(2 * share, share)],
            store_sems.at[slot],
        )
        for slot in range(N_DP)
    ]
    for copy in stores:
        copy.start()
    for copy in stores:
        copy.wait()


def forward_call(order, rows, cols, normed, grad_out, shards, share, col_blocks):
    tokens = normed.shape[0]
    grads = jax.ShapeDtypeStruct((CHIPS, 3 * share, BS, BS), BF)
    return pl.pallas_call(
        functools.partial(forward_kernel, share),
        out_shape=(
            jax.ShapeDtypeStruct((col_blocks, tokens, 2 * BS), F32),
            jax.ShapeDtypeStruct((col_blocks, tokens, BS), BF),
            grads,
            grads,
        ),
        in_specs=[spec(pltpu.SMEM)] * 3 + [spec(pltpu.VMEM)] * 2 + [spec(pl.ANY)] * N_DP,
        out_specs=(spec(pltpu.VMEM), spec(pltpu.VMEM), spec(pl.ANY), spec(pl.ANY)),
        scratch_shapes=[
            pltpu.VMEM((N_DP * share, BS, 2 * BS), BF),
            pltpu.VMEM((N_DP, share, BS, BS), BF),
            pltpu.SemaphoreType.DMA((N_DP, 2)),
            pltpu.SemaphoreType.DMA((N_DP,)),
        ],
        compiler_params=pltpu.CompilerParams(vmem_limit_bytes=VMEM_LIMIT),
        cost_estimate=pl.CostEstimate(flops=3 * 112 * 192 * 128 * 256, bytes_accessed=20_000_000, transcendentals=0),
        name="forward",
    )(order, rows, cols, normed, grad_out, *shards)


def backward_kernel(share, *refs):
    order, rows, cols, normed, grad_out, gate_up = refs[:6]
    shards = refs[6 : 6 + N_DP]
    mine, other, pre = refs[8 + N_DP : 11 + N_DP]
    held, grad_hidden, grads, load_sems, store_sems = refs[11 + N_DP :]
    copies = load_single(shards, held, load_sems, share)
    for copy in copies:
        copy.start()
    grad_hidden[...] = jnp.zeros_like(grad_hidden)
    for copy in copies:
        copy.wait()

    def back_hidden(slot, carry):
        base = order[slot] * share
        for j in range(share):
            row, col = rows[base + j], cols[base + j]
            grad_hidden[col] += mm_t(grad_out[:, lanes(row)], held[slot * share + j])
        return carry

    lax.fori_loop(0, N_DP, back_hidden, 0)

    def activate(col, carry):
        gate = gate_up[col, :, 0:BS]
        up = gate_up[col, :, BS:]
        back = grad_hidden[col]
        sig = 1.0 / (1.0 + jnp.exp(-gate))
        pre[col, :, 0:BS] = (back * up * sig * (1.0 + gate * (1.0 - sig))).astype(BF)
        pre[col, :, BS:] = (back * gate * sig).astype(BF)
        return carry

    lax.fori_loop(0, pre.shape[0], activate, 0)

    def weight_grad(slot, carry):
        base = order[slot] * share
        for j in range(share):
            row, col = rows[base + j], cols[base + j]
            both = mm_l(normed[:, lanes(row)], pre[col]).astype(BF)
            grads[slot, j] = both[:, 0:BS]
            grads[slot, share + j] = both[:, BS:]
        return carry

    lax.fori_loop(0, N_DP, weight_grad, 0)
    stores = [
        pltpu.make_async_copy(
            grads.at[slot],
            (mine if slot < CHIPS else other).at[slot % CHIPS, pl.ds(0, 2 * share)],
            store_sems.at[slot],
        )
        for slot in range(N_DP)
    ]
    for copy in stores:
        copy.start()
    for copy in stores:
        copy.wait()


def backward_call(order, rows, cols, normed, grad_out, gate_up, shards, mine, other, share):
    col_blocks, tokens, _ = gate_up.shape
    first = 6 + N_DP
    return pl.pallas_call(
        functools.partial(backward_kernel, share),
        out_shape=(
            jax.ShapeDtypeStruct(mine.shape, BF),
            jax.ShapeDtypeStruct(other.shape, BF),
            jax.ShapeDtypeStruct((col_blocks, tokens, 2 * BS), BF),
        ),
        in_specs=[spec(pltpu.SMEM)] * 3 + [spec(pltpu.VMEM)] * 3 + [spec(pl.ANY)] * (N_DP + 2),
        out_specs=(spec(pl.ANY), spec(pl.ANY), spec(pltpu.VMEM)),
        scratch_shapes=[
            pltpu.VMEM((N_DP * share, BS, BS), BF),
            pltpu.VMEM((col_blocks, tokens, BS), F32),
            pltpu.VMEM((N_DP, 2 * share, BS, BS), BF),
            pltpu.SemaphoreType.DMA((N_DP,)),
            pltpu.SemaphoreType.DMA((N_DP,)),
        ],
        input_output_aliases={first: 0, first + 1: 1},
        compiler_params=pltpu.CompilerParams(vmem_limit_bytes=VMEM_LIMIT),
        cost_estimate=pl.CostEstimate(flops=3 * 112 * 192 * 128 * 256, bytes_accessed=20_000_000, transcendentals=0),
        name="backward",
    )(order, rows, cols, normed, grad_out, gate_up, *shards, mine, other)


def input_kernel(share, *refs):
    order, rows, cols, place, index, weights, pre, stats, gain = refs[:9]
    history = refs[9]
    shards = refs[10 : 10 + N_DP]
    pieces = refs[10 + N_DP : 14 + N_DP]
    held, layers, total, load_sems, layer_sems = refs[14 + N_DP :]
    tokens, width = total.shape
    copies = load_pair(shards, held, load_sems, share)
    for copy in copies:
        copy.start()
    layer_copies = [
        pltpu.make_async_copy(history.at[index[slot]], layers.at[slot], layer_sems.at[slot]) for slot in range(4)
    ]
    for copy in layer_copies:
        copy.start()
    total[...] = jnp.zeros_like(total)
    for copy in copies:
        copy.wait()

    def back_input(slot, carry):
        base = order[slot] * share
        for j in range(share):
            row, col = rows[base + j], cols[base + j]
            total[:, lanes(row)] += mm_t(pre[col], held[slot * share + j])
        return carry

    lax.fori_loop(0, N_DP, back_input, 0)
    for copy in layer_copies:
        copy.wait()

    scale = stats[:, 0:1]
    zero = jnp.zeros((tokens, BS), F32)
    step = sign_of(place[0])
    x_here = place[1]
    offsets = (0, step, -step, 2)
    sums = [zero] * 4
    for way, piece in enumerate(pieces):
        x_there = (x_here + offsets[way] + 2 * N_X) % N_X
        for part in range(N_YLO):
            half = (part + place[2]) % N_YLO
            for block in range(piece.shape[2] // BS):
                where = lanes((x_there * N_YLO + half) * (piece.shape[2] // BS) + block)
                cut = pl.ds(block * BS, BS)
                value = total[:, where]
                piece[part, 0:tokens, cut] = value.astype(BF)
                scaled = value * gain[:, where]
                mixed = zero
                for slot in range(4):
                    layer = layers[slot, :, where].astype(F32)
                    sums[slot] = sums[slot] + scaled * layer
                    mixed = mixed + weights[slot] * layer
                row = jnp.sum(value * mixed * scale, axis=0, keepdims=True)
                at = lax.broadcasted_iota(jnp.int32, (EXTRA, BS), 0)
                piece[part, tokens : tokens + EXTRA, cut] = jnp.where(at == 0, row, 0.0).astype(BF)

    alphas = [jnp.sum(s, axis=1, keepdims=True) for s in sums]
    s_col = sum(weights[slot] * alphas[slot] for slot in range(4))
    wide = jnp.broadcast_to(s_col, (tokens, BS))
    s_row = jnp.transpose(wide)[0:1]
    lane = lax.broadcasted_iota(jnp.int32, (1, BS), 1)
    slots = jnp.zeros((1, BS), F32)
    source = place[1] * N_YLO + place[2]
    for slot in range(4):
        per_token = (
            scale * alphas[slot]
            - scale * scale * scale * stats[:, 1 + slot : 2 + slot] * s_col / width
            + stats[:, 5 + slot : 6 + slot] / N_TENSOR
        )
        value = jnp.sum(per_token, axis=0, keepdims=True)
        for term in range(3):
            rounded = value.astype(BF).astype(F32)
            slots = jnp.where(lane == source * 12 + slot * 3 + term, rounded, slots)
            value = value - rounded
    for piece in pieces:
        for part in range(N_YLO):
            for block in range(2):
                size = min(BS, tokens - block * BS)
                at = lax.broadcasted_iota(jnp.int32, (EXTRA, BS), 0)
                lead = s_row[:, block * BS : block * BS + size]
                if size < BS:
                    lead = jnp.concatenate([lead, jnp.zeros((1, BS - size), F32)], axis=1)
                old = piece[part, tokens : tokens + EXTRA, pl.ds(block * BS, BS)].astype(F32)
                new = jnp.where(at == 2, lead, old)
                if block == 0:
                    new = jnp.where(at == 1, slots, new)
                piece[part, tokens : tokens + EXTRA, pl.ds(block * BS, BS)] = new.astype(BF)


def input_call(order, rows, cols, place, depth_index, depth_weights, pre, stats, gain, history, shards, share):
    tokens = pre.shape[1]
    width = history.shape[2]
    piece = jax.ShapeDtypeStruct((N_YLO, tokens + EXTRA, width // N_TENSOR), BF)
    return pl.pallas_call(
        functools.partial(input_kernel, share),
        out_shape=(piece,) * N_X,
        in_specs=[spec(pltpu.SMEM)] * 6 + [spec(pltpu.VMEM)] * 3 + [spec(pl.ANY)] * (N_DP + 1),
        out_specs=(spec(pltpu.VMEM),) * N_X,
        scratch_shapes=[
            pltpu.VMEM((N_DP * share, BS, 2 * BS), BF),
            pltpu.VMEM((4, tokens, width), BF),
            pltpu.VMEM((tokens, width), F32),
            pltpu.SemaphoreType.DMA((N_DP, 2)),
            pltpu.SemaphoreType.DMA((4,)),
        ],
        compiler_params=pltpu.CompilerParams(vmem_limit_bytes=VMEM_LIMIT),
        cost_estimate=pl.CostEstimate(flops=2 * 112 * 192 * 128 * 256, bytes_accessed=20_000_000, transcendentals=0),
        name="input_grad",
    )(order, rows, cols, place, depth_index, depth_weights, pre, stats, gain.reshape(1, width), history, *shards)


def output_kernel(share, *refs):
    order, rows, cols, place, hidden = refs[:5]
    shards = refs[5 : 5 + N_DP]
    pieces = refs[5 + N_DP : 9 + N_DP]
    held, total, load_sems = refs[9 + N_DP :]
    copies = load_single(shards, held, load_sems, share)
    for copy in copies:
        copy.start()
    total[...] = jnp.zeros_like(total)
    for copy in copies:
        copy.wait()

    def forward(slot, carry):
        base = order[slot] * share
        for j in range(share):
            row, col = rows[base + j], cols[base + j]
            total[:, lanes(row)] += mm(hidden[col], held[slot * share + j])
        return carry

    lax.fori_loop(0, N_DP, forward, 0)
    step = sign_of(place[0])
    offsets = (0, step, -step, 2)
    for way, piece in enumerate(pieces):
        x_there = (place[1] + offsets[way] + 2 * N_X) % N_X
        for part in range(N_YLO):
            half = (part + place[2]) % N_YLO
            size = piece.shape[2]
            piece[part] = total[:, lanes(x_there * N_YLO + half, size)].astype(BF)


def output_call(order, rows, cols, place, hidden, shards, share, width):
    tokens = hidden.shape[1]
    piece = jax.ShapeDtypeStruct((N_YLO, tokens, width // N_TENSOR), BF)
    return pl.pallas_call(
        functools.partial(output_kernel, share),
        out_shape=(piece,) * N_X,
        in_specs=[spec(pltpu.SMEM)] * 4 + [spec(pltpu.VMEM)] + [spec(pl.ANY)] * N_DP,
        out_specs=(spec(pltpu.VMEM),) * N_X,
        scratch_shapes=[
            pltpu.VMEM((N_DP * share, BS, BS), BF),
            pltpu.VMEM((tokens, width), F32),
            pltpu.SemaphoreType.DMA((N_DP,)),
        ],
        compiler_params=pltpu.CompilerParams(vmem_limit_bytes=VMEM_LIMIT),
        cost_estimate=pl.CostEstimate(flops=112 * 192 * 128 * 256, bytes_accessed=10_000_000, transcendentals=0),
        name="output",
    )(order, rows, cols, place, hidden, *shards)


def gather_dp(own):
    y_own = over_dp(own, "y")
    first_a, first_b = over_dp(own, "a"), over_dp(own, "b")
    second = over_dp(first_a, "a")
    y_a, y_b = over_dp(y_own, "a"), over_dp(y_own, "b")
    y_second = over_dp(second, "y")
    here = [own, y_own, first_a, first_b, second, y_a, y_b, y_second]
    return here + [over_dp(value, "c") for value in here]


def add(*values):
    return sum(v.astype(F32) for v in values)


def reduce_dp(mine, other):
    arrived = over_dp(other, "c")
    part = [add(mine[k], arrived[k]) for k in range(CHIPS)]
    low = [p.astype(BF) for p in part]
    far = add(part[A2], over_dp(low[Y2], "y")).astype(BF)
    near = add(part[B1], over_dp(far, "a")).astype(BF)
    across = add(part[YY], over_dp(low[YB], "a"), over_dp(low[YA], "b")).astype(BF)
    return add(part[OWN], over_dp(low[A1], "b"), over_dp(near, "a"), over_dp(across, "y"))


def reduce_tensor(pieces):
    own, to_a, to_b, far = pieces
    near = add(to_a, over_tensor(far, "a")).astype(BF)
    total = add(own, over_tensor(near, "a"), over_tensor(to_b, "b"))
    return add(total[0], over_tensor(total[1].astype(BF), "y"))


def per_device(
    history,
    depth_weights,
    depth_index,
    gain,
    gate_blocks,
    up_blocks,
    down_blocks,
    block_ids,
    grad_out,
):
    tokens, width = grad_out.shape
    share = gate_blocks.shape[0]
    col_blocks = 14
    share_width = width // N_TENSOR
    dp = lax.axis_index("dp")
    tensor = lax.axis_index("tensor")
    core = dp % N_CORE
    share_start = tensor * share_width

    slot = jnp.arange(N_DP, dtype=jnp.int32)
    flip = slot // CHIPS
    chip = slot % CHIPS
    ahead = jnp.where((chip == A1) | (chip == YA), -1, jnp.where((chip == B1) | (chip == YB), 1, 0))
    ahead = jnp.where((chip == A2) | (chip == Y2), 2, ahead)
    turn = ((chip == YY) | (chip >= YA)).astype(jnp.int32)
    there = (core + flip) % N_CORE
    order = (
        ((dp // (N_Y * N_CORE) + ahead * sign_of(there) + 2 * N_Z) % N_Z) * (N_Y * N_CORE)
        + ((dp // N_CORE + turn) % N_Y) * N_CORE
        + there
    ).astype(jnp.int32)
    rows, cols = block_ids[:, 0], block_ids[:, 1]
    where = jnp.arange(4, dtype=jnp.int32)
    place = jnp.where(where == 0, core, jnp.where(where == 1, tensor // N_YLO, tensor % N_YLO)).astype(jnp.int32)

    pair = gather_dp(jnp.concatenate([gate_blocks, up_blocks], axis=0))
    single = gather_dp(down_blocks)
    normed, stats = norm_call(depth_index, depth_weights, history, grad_out, gain)
    gate_up, hidden, mine, other = forward_call(
        order, rows, cols, normed, grad_out, pair, share, col_blocks
    )
    mine, other, pre = backward_call(
        order, rows, cols, normed, grad_out, gate_up, single, mine, other, share
    )
    block_grads = reduce_dp(mine, other)
    back_pieces = input_call(
        order, rows, cols, place, depth_index, depth_weights, pre, stats, gain, history, pair, share
    )
    out_pieces = output_call(order, rows, cols, place, hidden, single, share, width)
    back = reduce_tensor(back_pieces)
    ffn = reduce_tensor(out_pieces)

    history_share = lax.dynamic_slice_in_dim(history, share_start, share_width, 2)
    mixed = jnp.zeros((tokens, share_width), F32)
    for slot_index in range(4):
        earlier = lax.dynamic_index_in_dim(history_share, depth_index[slot_index], 0, keepdims=False)
        mixed = mixed + depth_weights[slot_index] * earlier.astype(F32)
    layer_out = (mixed + ffn).astype(BF)

    scale = stats[:, 0:1]
    gain_share = lax.dynamic_slice_in_dim(gain, share_start, share_width, 0)
    cot = lax.dynamic_slice_in_dim(grad_out, share_start, share_width, 1).astype(F32)
    s_col = back[tokens + 2, 0:tokens].reshape(tokens, 1)
    grad_mixed = cot + scale * gain_share * back[0:tokens] - mixed * (scale * scale * scale) * (s_col / width)

    depth = back[tokens + 1, 0 : N_TENSOR * 12].reshape(N_TENSOR, 4, 3)
    depth = depth.sum(axis=(0, 2))
    small = jnp.concatenate([back[tokens], depth, jnp.zeros((BS - 4,), F32)]).reshape(-1, BS)
    for kind in ("c", "y", "z1", "z2"):
        small = small + over_dp(small, kind)
    return (
        layer_out,
        grad_mixed,
        block_grads[0:share],
        block_grads[share : 2 * share],
        block_grads[2 * share :],
        small[share_width // BS, 0:4],
        small[0 : share_width // BS].reshape(share_width),
    )


def solution(mesh):
    placed = (
        P(None, "dp", None),
        P(),
        P(),
        P(),
        P(("tensor", "dp"), None, None),
        P(("tensor", "dp"), None, None),
        P(("tensor", "dp"), None, None),
        P("tensor", None),
        P("dp", None),
    )
    return jax.shard_map(
        per_device,
        mesh=mesh,
        in_specs=placed,
        out_specs=(
            P("dp", "tensor"),
            P("dp", "tensor"),
            P(("tensor", "dp"), None, None),
            P(("tensor", "dp"), None, None),
            P(("tensor", "dp"), None, None),
            P(),
            P("tensor"),
        ),
        check_vma=False,
    )
```

```python
import functools

import jax
import jax.numpy as jnp
from jax import lax
from jax.experimental import pallas as pl
from jax.experimental.pallas import tpu as pltpu
from jax.sharding import PartitionSpec as P


EPSILON = 1e-05
BS = 128
N_Z, N_Y, N_CORE = 4, 2, 2
N_X, N_YLO = 4, 2
N_DP = N_Z * N_Y * N_CORE
N_TENSOR = N_X * N_YLO
CHIPS = N_Z * N_Y
OWN, YY, A1, B1, A2, YA, YB, Y2 = range(8)
AHEAD = (0, 0, -1, 1, 2, -1, 1, 2)
TURN = (0, 1, 0, 0, 0, 1, 1, 1)
EARLY = [(chip, flip) for chip in (OWN, A1, B1, YY) for flip in range(2)]
LATE = [(chip, flip) for chip in (A2, YA, YB, Y2) for flip in range(2)]
FIRST = (Y2, YB, YA, A1)
SECOND = (A2, B1, YY, OWN)
FIRST_SLOTS = [(chip, flip) for chip in FIRST for flip in range(2)]
SECOND_SLOTS = [(chip, flip) for chip in SECOND for flip in range(2)]
TABLE = EARLY + LATE + FIRST_SLOTS + SECOND_SLOTS
AT_EARLY, AT_LATE, AT_FIRST, AT_SECOND = 0, 8, 16, 24
EXTRA = 16
TILE = 16
ROWS = 32
VMEM_LIMIT = 60 * 1024 * 1024


BF = jnp.bfloat16
F32 = jnp.float32


def sign_of(core):
    return 1 - 2 * core


def dp_perm(kind):
    pairs = []
    for z in range(N_Z):
        for y in range(N_Y):
            for core in range(N_CORE):
                tz, ty, tc = z, y, core
                if kind == "a":
                    tz = (z + sign_of(core)) % N_Z
                elif kind == "b":
                    tz = (z - sign_of(core)) % N_Z
                elif kind == "y":
                    ty = 1 - y
                elif kind == "c":
                    tc = 1 - core
                elif kind == "z1":
                    tz = z ^ 1
                elif kind == "z2":
                    tz = z ^ 2
                elif kind == "z3":
                    tz = z ^ 3
                elif kind == "yc":
                    ty, tc = 1 - y, 1 - core
                pairs.append(((z * N_Y + y) * N_CORE + core, (tz * N_Y + ty) * N_CORE + tc))
    return pairs


def tensor_perm(kind):
    pairs = []
    for dp in range(N_DP):
        step = sign_of(dp % N_CORE)
        for x in range(N_X):
            for ylo in range(N_YLO):
                tx, ty = x, ylo
                if kind == "a":
                    tx = (x + step) % N_X
                elif kind == "b":
                    tx = (x - step) % N_X
                elif kind == "y":
                    ty = 1 - ylo
                else:
                    tx = x ^ int(kind)
                pairs.append((dp * N_TENSOR + x * N_YLO + ylo, dp * N_TENSOR + tx * N_YLO + ty))
    return pairs


def over_dp(value, kind):
    return lax.ppermute(value, "dp", dp_perm(kind))


def over_tensor(value, kind):
    return lax.ppermute(value, ("dp", "tensor"), tensor_perm(kind))


def spec(space):
    return pl.BlockSpec(memory_space=space)


def lanes(index, size=BS):
    return pl.ds(pl.multiple_of(index * size, size), size)


def mm(left, right):
    return jnp.dot(left, right, preferred_element_type=F32)


def mm_t(left, right):
    return lax.dot_general(left, right, (((1,), (1,)), ((), ())), preferred_element_type=F32)


def mm_l(left, right):
    return lax.dot_general(left, right, (((0,), (0,)), ((), ())), preferred_element_type=F32)


def fold(value):
    return sum(value[:, k * BS : (k + 1) * BS] for k in range(value.shape[1] // BS))


def norm_kernel(index, weights, h0, h1, h2, h3, grad_out, gain, normed, stats, kept):
    tile, width = normed.shape
    size = 512
    zero = jnp.zeros((tile, BS), F32)
    squares, moments, cots = zero, [zero] * 4, [zero] * 4
    for at in range(0, width, size):
        cut = slice(at, at + size)
        layers = [h[0, :, cut].astype(F32) for h in (h0, h1, h2, h3)]
        mixed = weights[0] * layers[0]
        for slot in range(1, 4):
            mixed = mixed + weights[slot] * layers[slot]
        kept[:, cut] = mixed
        squares = squares + fold(mixed * mixed)
        cot = grad_out[:, cut].astype(F32)
        for slot in range(4):
            moments[slot] = moments[slot] + fold(mixed * layers[slot])
            cots[slot] = cots[slot] + fold(cot * layers[slot])
    scale = lax.rsqrt(jnp.sum(squares, axis=-1, keepdims=True) / width + EPSILON)
    for at in range(0, width, size):
        cut = slice(at, at + size)
        normed[:, cut] = (kept[:, cut] * scale * gain[:, cut]).astype(BF)
    lane = lax.broadcasted_iota(jnp.int32, stats.shape, 1)
    found = jnp.where(lane == 0, scale, 0.0)
    for slot in range(4):
        found = jnp.where(lane == 1 + slot, jnp.sum(moments[slot], axis=-1, keepdims=True), found)
        found = jnp.where(lane == 5 + slot, jnp.sum(cots[slot], axis=-1, keepdims=True), found)
    stats[...] = found


def norm_call(depth_index, depth_weights, history, grad_out, gain):
    tokens, width = grad_out.shape

    def layer_spec(slot):
        return pl.BlockSpec((1, TILE, width), lambda i, index: (index[slot], i, 0))

    return pl.pallas_call(
        norm_kernel,
        out_shape=(
            jax.ShapeDtypeStruct((tokens, width), BF),
            jax.ShapeDtypeStruct((tokens, BS), F32),
            jax.ShapeDtypeStruct((tokens, width), F32),
        ),
        grid_spec=pltpu.PrefetchScalarGridSpec(
            num_scalar_prefetch=1,
            grid=(tokens // TILE,),
            in_specs=[spec(pltpu.SMEM)]
            + [layer_spec(slot) for slot in range(4)]
            + [
                pl.BlockSpec((TILE, width), lambda i, index: (i, 0)),
                pl.BlockSpec((1, width), lambda i, index: (0, 0)),
            ],
            out_specs=[
                pl.BlockSpec((TILE, width), lambda i, index: (i, 0)),
                pl.BlockSpec((TILE, BS), lambda i, index: (i, 0)),
                pl.BlockSpec((TILE, width), lambda i, index: (i, 0)),
            ],
        ),
        compiler_params=pltpu.CompilerParams(vmem_limit_bytes=VMEM_LIMIT),
        cost_estimate=pl.CostEstimate(flops=tokens * width * 30, bytes_accessed=tokens * width * 12, transcendentals=0),
        name="norm",
    )(depth_index, depth_weights, history, history, history, history, grad_out, gain.reshape(1, width))


def join_kernel(gate, up, down, out, sems):
    share = gate.shape[0]
    copies = [
        pltpu.make_async_copy(ref, out.at[pl.ds(k * share, share)], sems.at[k])
        for k, ref in enumerate((gate, up, down))
    ]
    for copy in copies:
        copy.start()
    for copy in copies:
        copy.wait()


def join_call(gate, up, down):
    return pl.pallas_call(
        join_kernel,
        out_shape=jax.ShapeDtypeStruct((3 * gate.shape[0], BS, BS), BF),
        in_specs=[spec(pl.ANY)] * 3,
        out_specs=spec(pltpu.VMEM),
        scratch_shapes=[pltpu.SemaphoreType.DMA((3,))],
        name="join",
    )(gate, up, down)


def part_copies(shard, held, sems, share, parts, slot):
    here = pl.ds(slot * share, share)
    return [
        pltpu.make_async_copy(
            shard.at[pl.ds(part * share, share)], held.at[here, :, pl.ds(k * BS, BS)], sems.at[slot, k]
        )
        for k, part in enumerate(parts)
    ]


def start_parts(shards, held, sems, share, parts):
    for slot, shard in enumerate(shards):
        for copy in part_copies(shard, held, sems, share, parts, slot):
            copy.start()


def wait_parts(shards, held, sems, share, parts, slot):
    for copy in part_copies(shards[0], held, sems, share, parts, slot):
        copy.wait()


def shard_copies(shard, held_pair, held_down, sems, slot, share):
    here = pl.ds(slot * share, share)
    return [
        pltpu.make_async_copy(shard.at[pl.ds(0, share)], held_pair.at[here, :, pl.ds(0, BS)], sems.at[slot, 0]),
        pltpu.make_async_copy(shard.at[pl.ds(share, share)], held_pair.at[here, :, pl.ds(BS, BS)], sems.at[slot, 1]),
        pltpu.make_async_copy(shard.at[pl.ds(2 * share, share)], held_down.at[here], sems.at[slot, 2]),
    ]


def start_shards(shards, held_pair, held_down, sems, share):
    for slot, shard in enumerate(shards):
        for copy in shard_copies(shard, held_pair, held_down, sems, slot, share):
            copy.start()


def accumulate(share, at, table, rows, cols, normed, grad_out, shards, held_pair, held_down, sems, gate_up, back):
    def one_slot(slot, carry):
        for copy in shard_copies(shards[0], held_pair, held_down, sems, slot, share):
            copy.wait()
        base = table[at + slot] * share
        for j in range(share):
            row, col = rows[base + j], cols[base + j]
            gate_up[col] += mm(normed[:, lanes(row)], held_pair[slot * share + j])
            back[col] += mm_t(grad_out[:, lanes(row)], held_down[slot * share + j])
        return carry

    lax.fori_loop(0, len(shards), one_slot, 0)


def weight_grads(share, at, table, rows, cols, normed, grad_out, hidden, pre, grads, mine, other, sems):
    def stores(chip):
        return [
            pltpu.make_async_copy(grads.at[chip, 0], mine.at[chip], sems.at[chip, 0]),
            pltpu.make_async_copy(grads.at[chip, 1], other.at[chip], sems.at[chip, 1]),
        ]

    def one_chip(chip, carry):
        for flip in range(2):
            base = table[at + chip * 2 + flip] * share
            for j in range(share):
                row, col = rows[base + j], cols[base + j]
                both = mm_l(normed[:, lanes(row)], pre[col]).astype(BF)
                grads[chip, flip, j] = both[:, 0:BS]
                grads[chip, flip, share + j] = both[:, BS:]
                grads[chip, flip, 2 * share + j] = mm_l(hidden[col], grad_out[:, lanes(row)]).astype(BF)
            stores(chip)[flip].start()
        return carry

    lax.fori_loop(0, mine.shape[0], one_chip, 0)
    for chip in range(mine.shape[0]):
        for copy in stores(chip):
            copy.wait()


def early_kernel(share, count, *refs):
    table, rows, cols, normed, grad_out = refs[:5]
    shards = refs[5 : 5 + count]
    gate_up, back = refs[5 + count : 7 + count]
    held_pair, held_down, sems = refs[7 + count :]
    start_shards(shards, held_pair, held_down, sems, share)
    gate_up[...] = jnp.zeros_like(gate_up)
    back[...] = jnp.zeros_like(back)
    accumulate(
        share, AT_EARLY, table, rows, cols, normed, grad_out, shards, held_pair, held_down, sems, gate_up, back
    )


def early_call(table, rows, cols, normed, grad_out, shards, share, col_blocks):
    tokens = normed.shape[0]
    count = len(shards)
    return pl.pallas_call(
        functools.partial(early_kernel, share, count),
        out_shape=(
            jax.ShapeDtypeStruct((col_blocks, tokens, 2 * BS), F32),
            jax.ShapeDtypeStruct((col_blocks, tokens, BS), F32),
        ),
        in_specs=[spec(pltpu.SMEM)] * 3 + [spec(pltpu.VMEM)] * 2 + [spec(pl.ANY)] * count,
        out_specs=(spec(pltpu.VMEM), spec(pltpu.VMEM)),
        scratch_shapes=[
            pltpu.VMEM((count * share, BS, 2 * BS), BF),
            pltpu.VMEM((count * share, BS, BS), BF),
            pltpu.SemaphoreType.DMA((count, 3)),
        ],
        compiler_params=pltpu.CompilerParams(vmem_limit_bytes=VMEM_LIMIT),
        cost_estimate=pl.CostEstimate(flops=3 * 56 * 192 * 128 * 256, bytes_accessed=12_000_000, transcendentals=0),
        name="early",
    )(table, rows, cols, normed, grad_out, *shards)


def late_kernel(share, count, *refs):
    table, rows, cols, normed, grad_out, gate_up_in, back_in = refs[:7]
    shards = refs[7 : 7 + count]
    hidden, pre, mine, other = refs[7 + count : 11 + count]
    held_pair, held_down, gate_up, back, grads, sems, store_sems = refs[11 + count :]
    start_shards(shards, held_pair, held_down, sems, share)
    gate_up[...] = gate_up_in[...]
    back[...] = back_in[...]
    accumulate(
        share, AT_LATE, table, rows, cols, normed, grad_out, shards, held_pair, held_down, sems, gate_up, back
    )

    def activate(col, carry):
        gate = gate_up[col, :, 0:BS]
        up = gate_up[col, :, BS:]
        cot = back[col]
        sig = 1.0 / (1.0 + jnp.exp(-gate))
        act = gate * sig
        hidden[col] = (act * up).astype(BF)
        pre[col, :, 0:BS] = (cot * up * sig * (1.0 + gate * (1.0 - sig))).astype(BF)
        pre[col, :, BS:] = (cot * act).astype(BF)
        return carry

    lax.fori_loop(0, hidden.shape[0], activate, 0)
    weight_grads(
        share, AT_FIRST, table, rows, cols, normed, grad_out, hidden, pre, grads, mine, other, store_sems
    )


def late_call(table, rows, cols, normed, grad_out, gate_up, back, shards, share):
    col_blocks, tokens, _ = gate_up.shape
    count = len(shards)
    half = CHIPS // 2
    grads = jax.ShapeDtypeStruct((half, 3 * share, BS, BS), BF)
    return pl.pallas_call(
        functools.partial(late_kernel, share, count),
        out_shape=(
            jax.ShapeDtypeStruct((col_blocks, tokens, BS), BF),
            jax.ShapeDtypeStruct((col_blocks, tokens, 2 * BS), BF),
            grads,
            grads,
        ),
        in_specs=[spec(pltpu.SMEM)] * 3 + [spec(pltpu.VMEM)] * 4 + [spec(pl.ANY)] * count,
        out_specs=(spec(pltpu.VMEM), spec(pltpu.VMEM), spec(pl.ANY), spec(pl.ANY)),
        scratch_shapes=[
            pltpu.VMEM((count * share, BS, 2 * BS), BF),
            pltpu.VMEM((count * share, BS, BS), BF),
            pltpu.VMEM((col_blocks, tokens, 2 * BS), F32),
            pltpu.VMEM((col_blocks, tokens, BS), F32),
            pltpu.VMEM((half, 2, 3 * share, BS, BS), BF),
            pltpu.SemaphoreType.DMA((count, 3)),
            pltpu.SemaphoreType.DMA((half, 2)),
        ],
        compiler_params=pltpu.CompilerParams(vmem_limit_bytes=VMEM_LIMIT),
        cost_estimate=pl.CostEstimate(flops=6 * 56 * 192 * 128 * 256, bytes_accessed=20_000_000, transcendentals=0),
        name="late",
    )(table, rows, cols, normed, grad_out, gate_up, back, *shards)


def rest_kernel(share, table, rows, cols, normed, grad_out, hidden, pre, mine, other, grads, store_sems):
    weight_grads(
        share, AT_SECOND, table, rows, cols, normed, grad_out, hidden, pre, grads, mine, other, store_sems
    )


def rest_call(table, rows, cols, normed, grad_out, hidden, pre, share):
    half = CHIPS // 2
    grads = jax.ShapeDtypeStruct((half, 3 * share, BS, BS), BF)
    return pl.pallas_call(
        functools.partial(rest_kernel, share),
        out_shape=(grads, grads),
        in_specs=[spec(pltpu.SMEM)] * 3 + [spec(pltpu.VMEM)] * 4,
        out_specs=(spec(pl.ANY), spec(pl.ANY)),
        scratch_shapes=[
            pltpu.VMEM((half, 2, 3 * share, BS, BS), BF),
            pltpu.SemaphoreType.DMA((half, 2)),
        ],
        compiler_params=pltpu.CompilerParams(vmem_limit_bytes=VMEM_LIMIT),
        cost_estimate=pl.CostEstimate(flops=3 * 56 * 192 * 128 * 256, bytes_accessed=10_000_000, transcendentals=0),
        name="rest",
    )(table, rows, cols, normed, grad_out, hidden, pre)


def input_kernel(share, *refs):
    order, rows, cols, place, index, weights, pre, stats, gain = refs[:9]
    history = refs[9]
    shards = refs[10 : 10 + N_DP]
    pieces = refs[10 + N_DP : 14 + N_DP]
    small = refs[14 + N_DP]
    held, layers, total, s_wide, load_sems, layer_sems = refs[15 + N_DP :]
    tokens, width = total.shape
    start_parts(shards, held, load_sems, share, (0, 1))
    layer_copies = [
        pltpu.make_async_copy(history.at[index[slot]], layers.at[slot], layer_sems.at[slot]) for slot in range(4)
    ]
    for copy in layer_copies:
        copy.start()
    total[...] = jnp.zeros_like(total)

    def back_input(slot, carry):
        wait_parts(shards, held, load_sems, share, (0, 1), slot)
        base = order[slot] * share
        for j in range(share):
            row, col = rows[base + j], cols[base + j]
            total[:, lanes(row)] += mm_t(pre[col], held[slot * share + j])
        return carry

    lax.fori_loop(0, N_DP, back_input, 0)
    for copy in layer_copies:
        copy.wait()

    step = sign_of(place[0])
    offsets = (0, step, -step, 2)
    per_part = pieces[0].shape[2] // BS
    small[...] = jnp.zeros_like(small)
    lane = lax.broadcasted_iota(jnp.int32, (1, BS), 1)

    def finish(chunk, carry):
        here = pl.ds(pl.multiple_of(chunk * ROWS, ROWS), ROWS)
        stat = stats[here]
        scale = stat[:, 0:1]
        zero = jnp.zeros((ROWS, BS), F32)
        sums = [zero] * 4
        for way, piece in enumerate(pieces):
            x_there = (place[1] + offsets[way] + 2 * N_X) % N_X
            for part in range(N_YLO):
                half = (part + place[2]) % N_YLO
                for block in range(per_part):
                    row = (x_there * N_YLO + half) * per_part + block
                    where = lanes(row)
                    value = total[here, where]
                    piece[part, here, block * BS : (block + 1) * BS] = value.astype(BF)
                    scaled = value * gain[:, where]
                    mixed = zero
                    for slot in range(4):
                        layer = layers[slot, here, where].astype(F32)
                        sums[slot] = sums[slot] + scaled * layer
                        mixed = mixed + weights[slot] * layer
                    small[pl.ds(row, 1), :] += jnp.sum(value * mixed * scale, axis=0, keepdims=True)
        alphas = [jnp.sum(total_sum, axis=1, keepdims=True) for total_sum in sums]
        s_col = sum(weights[slot] * alphas[slot] for slot in range(4))
        s_wide[here] = jnp.broadcast_to(s_col, (ROWS, BS))
        depth = jnp.zeros((1, BS), F32)
        for slot in range(4):
            per_token = (
                scale * alphas[slot]
                - scale * scale * scale * stat[:, 1 + slot : 2 + slot] * s_col / width
                + stat[:, 5 + slot : 6 + slot] / N_TENSOR
            )
            depth = jnp.where(lane == slot, jnp.sum(per_token, axis=0, keepdims=True), depth)
        small[width // BS : width // BS + 1, :] += depth
        return carry

    lax.fori_loop(0, tokens // ROWS, finish, 0)
    s_row = jnp.transpose(s_wide[...])[0:1]
    for piece in pieces:
        for part in range(N_YLO):
            piece[part, tokens:] = jnp.zeros((EXTRA, piece.shape[2]), BF)
            for block in range(2):
                size = min(BS, tokens - block * BS)
                lead = jnp.broadcast_to(s_row[:, block * BS : block * BS + size], (EXTRA, size))
                piece[part, tokens:, block * BS : block * BS + size] = lead.astype(BF)


def input_call(order, rows, cols, place, depth_index, depth_weights, pre, stats, gain, history, shards, share):
    tokens = pre.shape[1]
    width = history.shape[2]
    piece = jax.ShapeDtypeStruct((N_YLO, tokens + EXTRA, width // N_TENSOR), BF)
    return pl.pallas_call(
        functools.partial(input_kernel, share),
        out_shape=(piece,) * N_X + (jax.ShapeDtypeStruct((width // BS + 8, BS), F32),),
        in_specs=[spec(pltpu.SMEM)] * 6 + [spec(pltpu.VMEM)] * 3 + [spec(pl.ANY)] * (N_DP + 1),
        out_specs=(spec(pltpu.VMEM),) * (N_X + 1),
        scratch_shapes=[
            pltpu.VMEM((N_DP * share, BS, 2 * BS), BF),
            pltpu.VMEM((4, tokens, width), BF),
            pltpu.VMEM((tokens, width), F32),
            pltpu.VMEM((tokens, BS), F32),
            pltpu.SemaphoreType.DMA((N_DP, 2)),
            pltpu.SemaphoreType.DMA((4,)),
        ],
        compiler_params=pltpu.CompilerParams(vmem_limit_bytes=VMEM_LIMIT),
        cost_estimate=pl.CostEstimate(flops=2 * 112 * 192 * 128 * 256, bytes_accessed=20_000_000, transcendentals=0),
        name="input_grad",
    )(order, rows, cols, place, depth_index, depth_weights, pre, stats, gain.reshape(1, width), history, *shards)


def output_kernel(share, *refs):
    order, rows, cols, place, hidden = refs[:5]
    shards = refs[5 : 5 + N_DP]
    pieces = refs[5 + N_DP : 9 + N_DP]
    held, total, load_sems = refs[9 + N_DP :]
    start_parts(shards, held, load_sems, share, (2,))
    total[...] = jnp.zeros_like(total)

    def forward(slot, carry):
        wait_parts(shards, held, load_sems, share, (2,), slot)
        base = order[slot] * share
        for j in range(share):
            row, col = rows[base + j], cols[base + j]
            total[:, lanes(row)] += mm(hidden[col], held[slot * share + j])
        return carry

    lax.fori_loop(0, N_DP, forward, 0)
    step = sign_of(place[0])
    offsets = (0, step, -step, 2)
    for way, piece in enumerate(pieces):
        x_there = (place[1] + offsets[way] + 2 * N_X) % N_X
        for part in range(N_YLO):
            half = (part + place[2]) % N_YLO
            size = piece.shape[2]
            piece[part] = total[:, lanes(x_there * N_YLO + half, size)].astype(BF)


def output_call(order, rows, cols, place, hidden, shards, share, width):
    tokens = hidden.shape[1]
    piece = jax.ShapeDtypeStruct((N_YLO, tokens, width // N_TENSOR), BF)
    return pl.pallas_call(
        functools.partial(output_kernel, share),
        out_shape=(piece,) * N_X,
        in_specs=[spec(pltpu.SMEM)] * 4 + [spec(pltpu.VMEM)] + [spec(pl.ANY)] * N_DP,
        out_specs=(spec(pltpu.VMEM),) * N_X,
        scratch_shapes=[
            pltpu.VMEM((N_DP * share, BS, BS), BF),
            pltpu.VMEM((tokens, width), F32),
            pltpu.SemaphoreType.DMA((N_DP, 1)),
        ],
        compiler_params=pltpu.CompilerParams(vmem_limit_bytes=VMEM_LIMIT),
        cost_estimate=pl.CostEstimate(flops=112 * 192 * 128 * 256, bytes_accessed=10_000_000, transcendentals=0),
        name="output",
    )(order, rows, cols, place, hidden, *shards)


def add(*values):
    return sum(v.astype(F32) for v in values)


def reduce_tensor(pieces):
    own, to_a, to_b, far = pieces
    near = add(to_a, over_tensor(far, "a")).astype(BF)
    total = add(own, over_tensor(near, "a"), over_tensor(to_b, "b"))
    return add(total[0], over_tensor(total[1].astype(BF), "y"))


def reduce_small(small):
    for kinds in (("z1", "z2", "z3"), ("c", "y", "yc")):
        one, two, three = [over_dp(small, kind) for kind in kinds]
        small = (small + one) + (two + three)
    for kind in ("1", "2", "y"):
        small = small + over_tensor(small, kind)
    return small


def per_device(
    history,
    depth_weights,
    depth_index,
    gain,
    gate_blocks,
    up_blocks,
    down_blocks,
    block_ids,
    grad_out,
):
    tokens, width = grad_out.shape
    share = gate_blocks.shape[0]
    col_blocks = 14
    share_width = width // N_TENSOR
    dp = lax.axis_index("dp")
    tensor = lax.axis_index("tensor")
    core = dp % N_CORE
    share_start = tensor * share_width

    ahead = jnp.array([AHEAD[chip] for chip, _ in TABLE], jnp.int32)
    turn = jnp.array([TURN[chip] for chip, _ in TABLE], jnp.int32)
    flip = jnp.array([f for _, f in TABLE], jnp.int32)
    there = (core + flip) % N_CORE
    table = (
        ((dp // (N_Y * N_CORE) + ahead * sign_of(there) + 2 * N_Z) % N_Z) * (N_Y * N_CORE)
        + ((dp // N_CORE + turn) % N_Y) * N_CORE
        + there
    ).astype(jnp.int32)
    rows, cols = block_ids[:, 0], block_ids[:, 1]
    where = jnp.arange(4, dtype=jnp.int32)
    place = jnp.where(where == 0, core, jnp.where(where == 1, tensor // N_YLO, tensor % N_YLO)).astype(jnp.int32)

    got = {}
    own = join_call(gate_blocks, up_blocks, down_blocks)
    got[OWN, 0] = own
    got[A1, 0] = over_dp(own, "a")
    got[B1, 0] = over_dp(own, "b")
    got[YY, 0] = over_dp(own, "y")
    normed, stats, kept = norm_call(depth_index, depth_weights, history, grad_out, gain)
    got[A2, 0] = over_dp(got[A1, 0], "a")
    got[YA, 0] = over_dp(got[YY, 0], "a")
    got[YB, 0] = over_dp(got[YY, 0], "b")
    got[Y2, 0] = over_dp(got[A2, 0], "y")
    for chip in range(CHIPS):
        got[chip, 1] = over_dp(got[chip, 0], "c")

    gate_up, back = early_call(
        table, rows, cols, normed, grad_out, [got[key] for key in EARLY], share, col_blocks
    )
    hidden, pre, mine1, other1 = late_call(
        table, rows, cols, normed, grad_out, gate_up, back, [got[key] for key in LATE], share
    )
    arrived1 = over_dp(other1, "c")
    mine2, other2 = rest_call(table, rows, cols, normed, grad_out, hidden, pre, share)
    arrived2 = over_dp(other2, "c")
    part = {}
    for k in range(CHIPS // 2):
        part[SECOND[k]] = add(mine2[k], arrived2[k])
    far_y = over_dp(add(mine1[0], arrived1[0]).astype(BF), "y")
    across_a = over_dp(add(mine1[1], arrived1[1]).astype(BF), "a")
    both_b = over_dp(add(mine1[2:4], arrived1[2:4]).astype(BF), "b")
    across_b, near_b = both_b[0], both_b[1]

    shards = [got[key] for key in EARLY + LATE]
    *back_pieces, small = input_call(
        table, rows, cols, place, depth_index, depth_weights, pre, stats, gain, history, shards, share
    )
    out_pieces = output_call(table, rows, cols, place, hidden, shards, share, width)

    mine_y, arrived_y, across_a, across_b = lax.optimization_barrier((mine2, arrived2, across_a, across_b))
    at = SECOND.index(YY)
    part[YY] = add(mine_y[at], arrived_y[at])
    far = add(part[A2], far_y).astype(BF)
    near = add(part[B1], over_dp(far, "a")).astype(BF)
    across = over_dp(add(part[YY], across_a, across_b).astype(BF), "y")
    near_a = over_dp(near, "a")
    own1, own2 = mine2[SECOND.index(OWN)], arrived2[SECOND.index(OWN)]
    block_grads = [
        add(*[v[k * share : (k + 1) * share] for v in (own1, own2, near_a, near_b, across)]) for k in range(3)
    ]

    back = reduce_tensor(back_pieces)
    ffn = reduce_tensor(out_pieces)
    small = reduce_small(small)

    mixed = lax.dynamic_slice_in_dim(kept, share_start, share_width, 1)
    layer_out = (mixed + ffn).astype(BF)

    scale = stats[:, 0:1]
    gain_share = lax.dynamic_slice_in_dim(gain, share_start, share_width, 0)
    cot = lax.dynamic_slice_in_dim(grad_out, share_start, share_width, 1).astype(F32)
    s_col = back[tokens, 0:tokens].reshape(tokens, 1)
    grad_mixed = cot + scale * gain_share * back[0:tokens] - mixed * (scale * scale * scale) * (s_col / width)

    return (
        layer_out,
        grad_mixed,
        block_grads[0],
        block_grads[1],
        block_grads[2],
        small[width // BS, 0:4],
        lax.dynamic_slice_in_dim(small, share_start // BS, share_width // BS, 0).reshape(share_width),
    )


def solution(mesh):
    placed = (
        P(None, "dp", None),
        P(),
        P(),
        P(),
        P(("tensor", "dp"), None, None),
        P(("tensor", "dp"), None, None),
        P(("tensor", "dp"), None, None),
        P("tensor", None),
        P("dp", None),
    )

    return jax.shard_map(
        per_device,
        mesh=mesh,
        in_specs=placed,
        out_specs=(
            P("dp", "tensor"),
            P("dp", "tensor"),
            P(("tensor", "dp"), None, None),
            P(("tensor", "dp"), None, None),
            P(("tensor", "dp"), None, None),
            P(),
            P("tensor"),
        ),
        check_vma=False,
    )
```

```python
import functools

import jax
import jax.numpy as jnp
from jax import lax
from jax.experimental import pallas as pl
from jax.experimental.pallas import tpu as pltpu
from jax.sharding import PartitionSpec as P


EPSILON = 1e-05
BS = 128
N_Z, N_Y, N_CORE = 4, 2, 2
N_X, N_YLO = 4, 2
N_DP = N_Z * N_Y * N_CORE
N_TENSOR = N_X * N_YLO
CHIPS = N_Z * N_Y
OWN, YY, A1, B1, A2, YA, YB, Y2 = range(8)
AHEAD = (0, 0, -1, 1, 2, -1, 1, 2)
TURN = (0, 1, 0, 0, 0, 1, 1, 1)
EARLY = [(chip, flip) for chip in (OWN, A1, B1, YY, A2) for flip in range(2)]
LATE = [(chip, flip) for chip in (YA, YB, Y2) for flip in range(2)]
FIRST = (Y2, YB, YA, A1)
SECOND = (A2, B1, YY, OWN)
FIRST_SLOTS = [(chip, flip) for chip in FIRST for flip in range(2)]
SECOND_SLOTS = [(chip, flip) for chip in SECOND for flip in range(2)]
TABLE = EARLY + LATE + FIRST_SLOTS + SECOND_SLOTS
AT_EARLY, AT_LATE, AT_FIRST, AT_SECOND = 0, 10, 16, 24
EXTRA = 16
TILE = 64
ROWS = 32
MIB = 1024 * 1024


BF = jnp.bfloat16
F32 = jnp.float32


def sign_of(core):
    return 1 - 2 * core


def dp_perm(kind):
    pairs = []
    for z in range(N_Z):
        for y in range(N_Y):
            for core in range(N_CORE):
                tz, ty, tc = z, y, core
                if kind == "a":
                    tz = (z + sign_of(core)) % N_Z
                elif kind == "b":
                    tz = (z - sign_of(core)) % N_Z
                elif kind == "y":
                    ty = 1 - y
                elif kind == "c":
                    tc = 1 - core
                elif kind == "z1":
                    tz = z ^ 1
                elif kind == "z2":
                    tz = z ^ 2
                elif kind == "z3":
                    tz = z ^ 3
                elif kind == "yc":
                    ty, tc = 1 - y, 1 - core
                pairs.append(((z * N_Y + y) * N_CORE + core, (tz * N_Y + ty) * N_CORE + tc))
    return pairs


def tensor_perm(kind):
    pairs = []
    for dp in range(N_DP):
        step = sign_of(dp % N_CORE)
        for x in range(N_X):
            for ylo in range(N_YLO):
                tx, ty = x, ylo
                if kind == "a":
                    tx = (x + step) % N_X
                elif kind == "b":
                    tx = (x - step) % N_X
                elif kind == "y":
                    ty = 1 - ylo
                else:
                    tx = x ^ int(kind)
                pairs.append((dp * N_TENSOR + x * N_YLO + ylo, dp * N_TENSOR + tx * N_YLO + ty))
    return pairs


def over_dp(value, kind):
    return lax.ppermute(value, "dp", dp_perm(kind))


def over_tensor(value, kind):
    return lax.ppermute(value, ("dp", "tensor"), tensor_perm(kind))


def spec(space):
    return pl.BlockSpec(memory_space=space)


def lanes(index, size=BS):
    return pl.ds(pl.multiple_of(index * size, size), size)


def mm(left, right):
    return jnp.dot(left, right, preferred_element_type=F32)


def mm_t(left, right):
    return lax.dot_general(left, right, (((1,), (1,)), ((), ())), preferred_element_type=F32)


def mm_l(left, right):
    return lax.dot_general(left, right, (((0,), (0,)), ((), ())), preferred_element_type=F32)


def fold(value):
    return sum(value[:, k * BS : (k + 1) * BS] for k in range(value.shape[1] // BS))


def norm_kernel(index, weights, h0, h1, h2, h3, grad_out, gain, normed, stats, kept):
    tile, width = normed.shape
    size, rows = 512, 16

    def some_rows(step, carry):
        here = pl.ds(pl.multiple_of(step * rows, rows), rows)
        zero = jnp.zeros((rows, BS), F32)
        squares, moments, cots = zero, [zero] * 4, [zero] * 4
        for at in range(0, width, size):
            cut = slice(at, at + size)
            layers = [h[0, here, cut].astype(F32) for h in (h0, h1, h2, h3)]
            mixed = weights[0] * layers[0]
            for slot in range(1, 4):
                mixed = mixed + weights[slot] * layers[slot]
            kept[here, cut] = mixed
            squares = squares + fold(mixed * mixed)
            cot = grad_out[here, cut].astype(F32)
            for slot in range(4):
                moments[slot] = moments[slot] + fold(mixed * layers[slot])
                cots[slot] = cots[slot] + fold(cot * layers[slot])
        scale = lax.rsqrt(jnp.sum(squares, axis=-1, keepdims=True) / width + EPSILON)
        for at in range(0, width, size):
            cut = slice(at, at + size)
            normed[here, cut] = (kept[here, cut] * scale * gain[:, cut]).astype(BF)
        lane = lax.broadcasted_iota(jnp.int32, (rows, BS), 1)
        found = jnp.where(lane == 0, scale, 0.0)
        for slot in range(4):
            found = jnp.where(lane == 1 + slot, jnp.sum(moments[slot], axis=-1, keepdims=True), found)
            found = jnp.where(lane == 5 + slot, jnp.sum(cots[slot], axis=-1, keepdims=True), found)
        stats[here] = found
        return carry

    lax.fori_loop(0, tile // rows, some_rows, 0)


def norm_call(depth_index, depth_weights, history, grad_out, gain):
    tokens, width = grad_out.shape

    def layer_spec(slot):
        return pl.BlockSpec((1, TILE, width), lambda i, index: (index[slot], i, 0))

    return pl.pallas_call(
        norm_kernel,
        out_shape=(
            jax.ShapeDtypeStruct((tokens, width), BF),
            jax.ShapeDtypeStruct((tokens, BS), F32),
            jax.ShapeDtypeStruct((tokens, width), F32),
        ),
        grid_spec=pltpu.PrefetchScalarGridSpec(
            num_scalar_prefetch=1,
            grid=(tokens // TILE,),
            in_specs=[spec(pltpu.SMEM)]
            + [layer_spec(slot) for slot in range(4)]
            + [
                pl.BlockSpec((TILE, width), lambda i, index: (i, 0)),
                pl.BlockSpec((1, width), lambda i, index: (0, 0)),
            ],
            out_specs=[
                pl.BlockSpec((TILE, width), lambda i, index: (i, 0)),
                pl.BlockSpec((TILE, BS), lambda i, index: (i, 0)),
                pl.BlockSpec((TILE, width), lambda i, index: (i, 0)),
            ],
        ),
        compiler_params=pltpu.CompilerParams(vmem_limit_bytes=24 * MIB),
        cost_estimate=pl.CostEstimate(flops=tokens * width * 30, bytes_accessed=tokens * width * 12, transcendentals=0),
        name="norm",
    )(depth_index, depth_weights, history, history, history, history, grad_out, gain.reshape(1, width))


def join_kernel(gate, up, down, out, sems):
    share = gate.shape[0]
    copies = [
        pltpu.make_async_copy(ref, out.at[pl.ds(k * share, share)], sems.at[k])
        for k, ref in enumerate((gate, up, down))
    ]
    for copy in copies:
        copy.start()
    for copy in copies:
        copy.wait()


def join_call(gate, up, down):
    return pl.pallas_call(
        join_kernel,
        out_shape=jax.ShapeDtypeStruct((3 * gate.shape[0], BS, BS), BF),
        in_specs=[spec(pl.ANY)] * 3,
        out_specs=spec(pltpu.VMEM),
        scratch_shapes=[pltpu.SemaphoreType.DMA((3,))],
        name="join",
    )(gate, up, down)


def part_copies(shard, held, sems, share, parts, slot):
    here = pl.ds(slot * share, share)
    return [
        pltpu.make_async_copy(
            shard.at[pl.ds(part * share, share)], held.at[here, :, pl.ds(k * BS, BS)], sems.at[slot, k]
        )
        for k, part in enumerate(parts)
    ]


def start_parts(shards, held, sems, share, parts):
    for slot, shard in enumerate(shards):
        for copy in part_copies(shard, held, sems, share, parts, slot):
            copy.start()


def wait_parts(shards, held, sems, share, parts, slot):
    for copy in part_copies(shards[0], held, sems, share, parts, slot):
        copy.wait()


def shard_copies(shard, held_pair, held_down, sems, slot, share):
    here = pl.ds(slot * share, share)
    return [
        pltpu.make_async_copy(shard.at[pl.ds(0, share)], held_pair.at[here, :, pl.ds(0, BS)], sems.at[slot, 0]),
        pltpu.make_async_copy(shard.at[pl.ds(share, share)], held_pair.at[here, :, pl.ds(BS, BS)], sems.at[slot, 1]),
        pltpu.make_async_copy(shard.at[pl.ds(2 * share, share)], held_down.at[here], sems.at[slot, 2]),
    ]


def start_shards(shards, held_pair, held_down, sems, share):
    for slot, shard in enumerate(shards):
        for copy in shard_copies(shard, held_pair, held_down, sems, slot, share):
            copy.start()


def accumulate(share, at, table, rows, cols, normed, grad_out, shards, held_pair, held_down, sems, gate_up, back):
    def one_slot(slot, carry):
        for copy in shard_copies(shards[0], held_pair, held_down, sems, slot, share):
            copy.wait()
        base = table[at + slot] * share
        for j in range(share):
            row, col = rows[base + j], cols[base + j]
            gate_up[col] += mm(normed[:, lanes(row)], held_pair[slot * share + j])
            back[col] += mm_t(grad_out[:, lanes(row)], held_down[slot * share + j])
        return carry

    lax.fori_loop(0, len(shards), one_slot, 0)


def weight_grads(share, at, table, rows, cols, normed, grad_out, hidden, pre, grads, mine, other, sems):
    def stores(chip):
        return [
            pltpu.make_async_copy(grads.at[chip, 0], mine.at[chip], sems.at[chip, 0]),
            pltpu.make_async_copy(grads.at[chip, 1], other.at[chip], sems.at[chip, 1]),
        ]

    def one_chip(chip, carry):
        for flip in range(2):
            base = table[at + chip * 2 + flip] * share
            for j in range(share):
                row, col = rows[base + j], cols[base + j]
                both = mm_l(normed[:, lanes(row)], pre[col]).astype(BF)
                grads[chip, flip, j] = both[:, 0:BS]
                grads[chip, flip, share + j] = both[:, BS:]
                grads[chip, flip, 2 * share + j] = mm_l(hidden[col], grad_out[:, lanes(row)]).astype(BF)
            stores(chip)[flip].start()
        return carry

    lax.fori_loop(0, mine.shape[0], one_chip, 0)
    for chip in range(mine.shape[0]):
        for copy in stores(chip):
            copy.wait()


def early_kernel(share, count, *refs):
    table, rows, cols, normed, grad_out = refs[:5]
    shards = refs[5 : 5 + count]
    gate_up, back = refs[5 + count : 7 + count]
    held_pair, held_down, sems = refs[7 + count :]
    start_shards(shards, held_pair, held_down, sems, share)
    gate_up[...] = jnp.zeros_like(gate_up)
    back[...] = jnp.zeros_like(back)
    accumulate(
        share, AT_EARLY, table, rows, cols, normed, grad_out, shards, held_pair, held_down, sems, gate_up, back
    )


def early_call(table, rows, cols, normed, grad_out, shards, share, col_blocks):
    tokens = normed.shape[0]
    count = len(shards)
    return pl.pallas_call(
        functools.partial(early_kernel, share, count),
        out_shape=(
            jax.ShapeDtypeStruct((col_blocks, tokens, 2 * BS), F32),
            jax.ShapeDtypeStruct((col_blocks, tokens, BS), F32),
        ),
        in_specs=[spec(pltpu.SMEM)] * 3 + [spec(pltpu.VMEM)] * 2 + [spec(pl.ANY)] * count,
        out_specs=(spec(pltpu.VMEM), spec(pltpu.VMEM)),
        scratch_shapes=[
            pltpu.VMEM((count * share, BS, 2 * BS), BF),
            pltpu.VMEM((count * share, BS, BS), BF),
            pltpu.SemaphoreType.DMA((count, 3)),
        ],
        compiler_params=pltpu.CompilerParams(vmem_limit_bytes=18 * MIB),
        cost_estimate=pl.CostEstimate(flops=3 * 56 * 192 * 128 * 256, bytes_accessed=12_000_000, transcendentals=0),
        name="early",
    )(table, rows, cols, normed, grad_out, *shards)


def late_kernel(share, count, *refs):
    table, rows, cols, normed, grad_out, gate_up_in, back_in = refs[:7]
    shards = refs[7 : 7 + count]
    hidden, pre, mine, other = refs[7 + count : 11 + count]
    held_pair, held_down, gate_up, back, grads, sems, store_sems = refs[11 + count :]
    start_shards(shards, held_pair, held_down, sems, share)
    gate_up[...] = gate_up_in[...]
    back[...] = back_in[...]
    accumulate(
        share, AT_LATE, table, rows, cols, normed, grad_out, shards, held_pair, held_down, sems, gate_up, back
    )

    def activate(col, carry):
        gate = gate_up[col, :, 0:BS]
        up = gate_up[col, :, BS:]
        cot = back[col]
        sig = 1.0 / (1.0 + jnp.exp(-gate))
        act = gate * sig
        hidden[col] = (act * up).astype(BF)
        pre[col, :, 0:BS] = (cot * up * sig * (1.0 + gate * (1.0 - sig))).astype(BF)
        pre[col, :, BS:] = (cot * act).astype(BF)
        return carry

    lax.fori_loop(0, hidden.shape[0], activate, 0)
    weight_grads(
        share, AT_FIRST, table, rows, cols, normed, grad_out, hidden, pre, grads, mine, other, store_sems
    )


def late_call(table, rows, cols, normed, grad_out, gate_up, back, shards, share):
    col_blocks, tokens, _ = gate_up.shape
    count = len(shards)
    half = CHIPS // 2
    grads = jax.ShapeDtypeStruct((half, 3 * share, BS, BS), BF)
    return pl.pallas_call(
        functools.partial(late_kernel, share, count),
        out_shape=(
            jax.ShapeDtypeStruct((col_blocks, tokens, BS), BF),
            jax.ShapeDtypeStruct((col_blocks, tokens, 2 * BS), BF),
            grads,
            grads,
        ),
        in_specs=[spec(pltpu.SMEM)] * 3 + [spec(pltpu.VMEM)] * 4 + [spec(pl.ANY)] * count,
        out_specs=(spec(pltpu.VMEM), spec(pltpu.VMEM), spec(pl.ANY), spec(pl.ANY)),
        scratch_shapes=[
            pltpu.VMEM((count * share, BS, 2 * BS), BF),
            pltpu.VMEM((count * share, BS, BS), BF),
            pltpu.VMEM((col_blocks, tokens, 2 * BS), F32),
            pltpu.VMEM((col_blocks, tokens, BS), F32),
            pltpu.VMEM((half, 2, 3 * share, BS, BS), BF),
            pltpu.SemaphoreType.DMA((count, 3)),
            pltpu.SemaphoreType.DMA((half, 2)),
        ],
        compiler_params=pltpu.CompilerParams(vmem_limit_bytes=34 * MIB),
        cost_estimate=pl.CostEstimate(flops=6 * 56 * 192 * 128 * 256, bytes_accessed=20_000_000, transcendentals=0),
        name="late",
    )(table, rows, cols, normed, grad_out, gate_up, back, *shards)


def rest_kernel(share, table, rows, cols, normed, grad_out, hidden, pre, mine, other, grads, store_sems):
    weight_grads(
        share, AT_SECOND, table, rows, cols, normed, grad_out, hidden, pre, grads, mine, other, store_sems
    )


def rest_call(table, rows, cols, normed, grad_out, hidden, pre, share):
    half = CHIPS // 2
    grads = jax.ShapeDtypeStruct((half, 3 * share, BS, BS), BF)
    return pl.pallas_call(
        functools.partial(rest_kernel, share),
        out_shape=(grads, grads),
        in_specs=[spec(pltpu.SMEM)] * 3 + [spec(pltpu.VMEM)] * 4,
        out_specs=(spec(pl.ANY), spec(pl.ANY)),
        scratch_shapes=[
            pltpu.VMEM((half, 2, 3 * share, BS, BS), BF),
            pltpu.SemaphoreType.DMA((half, 2)),
        ],
        compiler_params=pltpu.CompilerParams(vmem_limit_bytes=16 * MIB),
        cost_estimate=pl.CostEstimate(flops=3 * 56 * 192 * 128 * 256, bytes_accessed=10_000_000, transcendentals=0),
        name="rest",
    )(table, rows, cols, normed, grad_out, hidden, pre)


def input_kernel(share, *refs):
    order, rows, cols, place, index, weights, pre, stats, gain = refs[:9]
    history = refs[9]
    shards = refs[10 : 10 + N_DP]
    pieces = refs[10 + N_DP : 14 + N_DP]
    small = refs[14 + N_DP]
    held, layers, total, s_wide, load_sems, layer_sems = refs[15 + N_DP :]
    tokens, width = total.shape
    start_parts(shards, held, load_sems, share, (0, 1))
    layer_copies = [
        pltpu.make_async_copy(history.at[index[slot]], layers.at[slot], layer_sems.at[slot]) for slot in range(4)
    ]
    for copy in layer_copies:
        copy.start()
    total[...] = jnp.zeros_like(total)

    def back_input(slot, carry):
        wait_parts(shards, held, load_sems, share, (0, 1), slot)
        base = order[slot] * share
        for j in range(share):
            row, col = rows[base + j], cols[base + j]
            total[:, lanes(row)] += mm_t(pre[col], held[slot * share + j])
        return carry

    lax.fori_loop(0, N_DP, back_input, 0)
    for copy in layer_copies:
        copy.wait()

    step = sign_of(place[0])
    offsets = (0, step, -step, 2)
    per_part = pieces[0].shape[2] // BS
    small[...] = jnp.zeros_like(small)
    lane = lax.broadcasted_iota(jnp.int32, (1, BS), 1)

    def finish(chunk, carry):
        here = pl.ds(pl.multiple_of(chunk * ROWS, ROWS), ROWS)
        stat = stats[here]
        scale = stat[:, 0:1]
        zero = jnp.zeros((ROWS, BS), F32)
        sums = [zero] * 4
        for way, piece in enumerate(pieces):
            x_there = (place[1] + offsets[way] + 2 * N_X) % N_X
            for part in range(N_YLO):
                half = (part + place[2]) % N_YLO
                for block in range(per_part):
                    row = (x_there * N_YLO + half) * per_part + block
                    where = lanes(row)
                    value = total[here, where]
                    piece[part, here, block * BS : (block + 1) * BS] = value.astype(BF)
                    scaled = value * gain[:, where]
                    mixed = zero
                    for slot in range(4):
                        layer = layers[slot, here, where].astype(F32)
                        sums[slot] = sums[slot] + scaled * layer
                        mixed = mixed + weights[slot] * layer
                    small[pl.ds(row, 1), :] += jnp.sum(value * mixed * scale, axis=0, keepdims=True)
        alphas = [jnp.sum(total_sum, axis=1, keepdims=True) for total_sum in sums]
        s_col = sum(weights[slot] * alphas[slot] for slot in range(4))
        s_wide[here] = jnp.broadcast_to(s_col, (ROWS, BS))
        depth = jnp.zeros((1, BS), F32)
        for slot in range(4):
            per_token = (
                scale * alphas[slot]
                - scale * scale * scale * stat[:, 1 + slot : 2 + slot] * s_col / width
                + stat[:, 5 + slot : 6 + slot] / N_TENSOR
            )
            depth = jnp.where(lane == slot, jnp.sum(per_token, axis=0, keepdims=True), depth)
        small[width // BS : width // BS + 1, :] += depth
        return carry

    lax.fori_loop(0, tokens // ROWS, finish, 0)
    s_row = jnp.transpose(s_wide[...])[0:1]
    for piece in pieces:
        for part in range(N_YLO):
            piece[part, tokens:] = jnp.zeros((EXTRA, piece.shape[2]), BF)
            for block in range(2):
                size = min(BS, tokens - block * BS)
                lead = jnp.broadcast_to(s_row[:, block * BS : block * BS + size], (EXTRA, size))
                piece[part, tokens:, block * BS : block * BS + size] = lead.astype(BF)


def input_call(order, rows, cols, place, depth_index, depth_weights, pre, stats, gain, history, shards, share):
    tokens = pre.shape[1]
    width = history.shape[2]
    piece = jax.ShapeDtypeStruct((N_YLO, tokens + EXTRA, width // N_TENSOR), BF)
    return pl.pallas_call(
        functools.partial(input_kernel, share),
        out_shape=(piece,) * N_X + (jax.ShapeDtypeStruct((width // BS + 8, BS), F32),),
        in_specs=[spec(pltpu.SMEM)] * 6 + [spec(pltpu.VMEM)] * 3 + [spec(pl.ANY)] * (N_DP + 1),
        out_specs=(spec(pltpu.VMEM),) * (N_X + 1),
        scratch_shapes=[
            pltpu.VMEM((N_DP * share, BS, 2 * BS), BF),
            pltpu.VMEM((4, tokens, width), BF),
            pltpu.VMEM((tokens, width), F32),
            pltpu.VMEM((tokens, BS), F32),
            pltpu.SemaphoreType.DMA((N_DP, 2)),
            pltpu.SemaphoreType.DMA((4,)),
        ],
        compiler_params=pltpu.CompilerParams(vmem_limit_bytes=30 * MIB),
        cost_estimate=pl.CostEstimate(flops=2 * 112 * 192 * 128 * 256, bytes_accessed=20_000_000, transcendentals=0),
        name="input_grad",
    )(order, rows, cols, place, depth_index, depth_weights, pre, stats, gain.reshape(1, width), history, *shards)


def output_kernel(share, *refs):
    order, rows, cols, place, hidden = refs[:5]
    shards = refs[5 : 5 + N_DP]
    pieces = refs[5 + N_DP : 9 + N_DP]
    held, total, load_sems = refs[9 + N_DP :]
    start_parts(shards, held, load_sems, share, (2,))
    total[...] = jnp.zeros_like(total)

    def forward(slot, carry):
        wait_parts(shards, held, load_sems, share, (2,), slot)
        base = order[slot] * share
        for j in range(share):
            row, col = rows[base + j], cols[base + j]
            total[:, lanes(row)] += mm(hidden[col], held[slot * share + j])
        return carry

    lax.fori_loop(0, N_DP, forward, 0)
    step = sign_of(place[0])
    offsets = (0, step, -step, 2)
    for way, piece in enumerate(pieces):
        x_there = (place[1] + offsets[way] + 2 * N_X) % N_X
        for part in range(N_YLO):
            half = (part + place[2]) % N_YLO
            size = piece.shape[2]
            piece[part] = total[:, lanes(x_there * N_YLO + half, size)].astype(BF)


def output_call(order, rows, cols, place, hidden, shards, share, width):
    tokens = hidden.shape[1]
    piece = jax.ShapeDtypeStruct((N_YLO, tokens, width // N_TENSOR), BF)
    return pl.pallas_call(
        functools.partial(output_kernel, share),
        out_shape=(piece,) * N_X,
        in_specs=[spec(pltpu.SMEM)] * 4 + [spec(pltpu.VMEM)] + [spec(pl.ANY)] * N_DP,
        out_specs=(spec(pltpu.VMEM),) * N_X,
        scratch_shapes=[
            pltpu.VMEM((N_DP * share, BS, BS), BF),
            pltpu.VMEM((tokens, width), F32),
            pltpu.SemaphoreType.DMA((N_DP, 1)),
        ],
        compiler_params=pltpu.CompilerParams(vmem_limit_bytes=16 * MIB),
        cost_estimate=pl.CostEstimate(flops=112 * 192 * 128 * 256, bytes_accessed=10_000_000, transcendentals=0),
        name="output",
    )(order, rows, cols, place, hidden, *shards)


def barrier(*values):
    return lax.optimization_barrier(values)


def add(*values):
    return sum(v.astype(F32) for v in values)


def reduce_tensor(pieces, after, last):
    own, to_a, to_b, far = pieces
    near = add(to_a, over_tensor(far, "a")).astype(BF)
    from_a, _ = barrier(over_tensor(near, "a"), after)
    total = add(own, from_a, over_tensor(to_b, "b"))
    moved, _ = barrier(over_tensor(total[1].astype(BF), "y"), last)
    return add(total[0], moved)


def reduce_small(small, after):
    small = small + over_dp(small, "c")
    small = small + over_dp(small, "y")
    moved, _ = barrier(over_tensor(small, "y"), after)
    small = small + moved
    one, two, three = [over_dp(small, kind) for kind in ("z1", "z2", "z3")]
    small = (small + one) + (two + three)
    one, two, three = [over_tensor(small, kind) for kind in ("1", "2", "3")]
    return (small + one) + (two + three)


def per_device(
    history,
    depth_weights,
    depth_index,
    gain,
    gate_blocks,
    up_blocks,
    down_blocks,
    block_ids,
    grad_out,
):
    tokens, width = grad_out.shape
    share = gate_blocks.shape[0]
    col_blocks = 14
    share_width = width // N_TENSOR
    dp = lax.axis_index("dp")
    tensor = lax.axis_index("tensor")
    core = dp % N_CORE
    share_start = tensor * share_width

    ahead = jnp.array([AHEAD[chip] for chip, _ in TABLE], jnp.int32)
    turn = jnp.array([TURN[chip] for chip, _ in TABLE], jnp.int32)
    flip = jnp.array([f for _, f in TABLE], jnp.int32)
    there = (core + flip) % N_CORE
    table = (
        ((dp // (N_Y * N_CORE) + ahead * sign_of(there) + 2 * N_Z) % N_Z) * (N_Y * N_CORE)
        + ((dp // N_CORE + turn) % N_Y) * N_CORE
        + there
    ).astype(jnp.int32)
    rows, cols = block_ids[:, 0], block_ids[:, 1]
    where = jnp.arange(4, dtype=jnp.int32)
    place = jnp.where(where == 0, core, jnp.where(where == 1, tensor // N_YLO, tensor % N_YLO)).astype(jnp.int32)

    got = {}
    own = join_call(gate_blocks, up_blocks, down_blocks)
    got[OWN, 0] = own
    got[A1, 0] = over_dp(own, "a")
    got[B1, 0] = over_dp(own, "b")
    got[YY, 0] = over_dp(own, "y")
    normed, stats, kept = norm_call(depth_index, depth_weights, history, grad_out, gain)
    got[A2, 0] = over_dp(got[A1, 0], "a")
    got[YA, 0] = over_dp(got[YY, 0], "a")
    got[YB, 0] = over_dp(got[YY, 0], "b")
    got[Y2, 0] = over_dp(got[A2, 0], "y")
    for chip in range(CHIPS):
        got[chip, 1] = over_dp(got[chip, 0], "c")

    gate_up, back = early_call(
        table, rows, cols, normed, grad_out, [got[key] for key in EARLY], share, col_blocks
    )
    hidden, pre, mine1, other1 = late_call(
        table, rows, cols, normed, grad_out, gate_up, back, [got[key] for key in LATE], share
    )
    arrived1 = over_dp(other1, "c")
    mine2, other2 = rest_call(table, rows, cols, normed, grad_out, hidden, pre, share)
    arrived2 = over_dp(other2, "c")
    part = {}
    for k in range(CHIPS // 2):
        part[SECOND[k]] = add(mine2[k], arrived2[k])
    far_y = over_dp(add(mine1[0], arrived1[0]).astype(BF), "y")
    across_a = over_dp(add(mine1[1], arrived1[1]).astype(BF), "a")
    both_b = over_dp(add(mine1[2:4], arrived1[2:4]).astype(BF), "b")

    shards = [got[key] for key in EARLY + LATE]
    *back_pieces, small = input_call(
        table, rows, cols, place, depth_index, depth_weights, pre, stats, gain, history, shards, share
    )
    out_pieces = output_call(table, rows, cols, place, hidden, shards, share, width)

    near_b = both_b[1]
    mine_y, arrived_y, across_a, across_b = barrier(mine2, arrived2, across_a, both_b)
    across_b = across_b[0]
    at = SECOND.index(YY)
    part[YY] = add(mine_y[at], arrived_y[at])
    far = add(part[A2], far_y).astype(BF)
    near = add(part[B1], over_dp(far, "a")).astype(BF)
    across_low = add(part[YY], across_a, across_b).astype(BF)
    across = over_dp(across_low, "y")
    near_a = over_dp(near, "a")
    own1, own2 = mine2[SECOND.index(OWN)], arrived2[SECOND.index(OWN)]
    block_grads = [
        add(*[v[k * share : (k + 1) * share] for v in (own1, own2, near_a, near_b, across)]) for k in range(3)
    ]

    back = reduce_tensor(back_pieces, near, block_grads[0])
    ffn = reduce_tensor(out_pieces, near, block_grads[0])
    small = reduce_small(small, across_low)

    mixed = lax.dynamic_slice_in_dim(kept, share_start, share_width, 1)
    layer_out = (mixed + ffn).astype(BF)

    scale = stats[:, 0:1]
    gain_share = lax.dynamic_slice_in_dim(gain, share_start, share_width, 0)
    cot = lax.dynamic_slice_in_dim(grad_out, share_start, share_width, 1).astype(F32)
    s_col = back[tokens, 0:tokens].reshape(tokens, 1)
    grad_mixed = cot + scale * gain_share * back[0:tokens] - mixed * (scale * scale * scale) * (s_col / width)

    return (
        layer_out,
        grad_mixed,
        block_grads[0],
        block_grads[1],
        block_grads[2],
        small[width // BS, 0:4],
        lax.dynamic_slice_in_dim(small, share_start // BS, share_width // BS, 0).reshape(share_width),
    )


def solution(mesh):
    placed = (
        P(None, "dp", None),
        P(),
        P(),
        P(),
        P(("tensor", "dp"), None, None),
        P(("tensor", "dp"), None, None),
        P(("tensor", "dp"), None, None),
        P("tensor", None),
        P("dp", None),
    )

    return jax.shard_map(
        per_device,
        mesh=mesh,
        in_specs=placed,
        out_specs=(
            P("dp", "tensor"),
            P("dp", "tensor"),
            P(("tensor", "dp"), None, None),
            P(("tensor", "dp"), None, None),
            P(("tensor", "dp"), None, None),
            P(),
            P("tensor"),
        ),
        check_vma=False,
    )
```

```python
import functools

import jax
import jax.numpy as jnp
from jax import lax
from jax.experimental import pallas as pl
from jax.experimental.pallas import tpu as pltpu
from jax.sharding import PartitionSpec as P


EPSILON = 1e-05
BS = 128
N_Z, N_Y, N_CORE = 4, 2, 2
N_X, N_YLO = 4, 2
N_DP = N_Z * N_Y * N_CORE
N_TENSOR = N_X * N_YLO
CHIPS = N_Z * N_Y
OWN, YY, A1, B1, A2, YA, YB, Y2 = range(8)
AHEAD = (0, 0, -1, 1, 2, -1, 1, 2)
TURN = (0, 1, 0, 0, 0, 1, 1, 1)
EARLY = [(chip, flip) for chip in (OWN, A1, B1, YY, A2) for flip in range(2)]
LATE = [(chip, flip) for chip in (YA, YB, Y2) for flip in range(2)]
FIRST = (Y2, YB, YA, A1)
SECOND = (A2, B1, YY, OWN)
FIRST_SLOTS = [(chip, flip) for chip in FIRST for flip in range(2)]
SECOND_SLOTS = [(chip, flip) for chip in SECOND for flip in range(2)]
TABLE = EARLY + LATE + FIRST_SLOTS + SECOND_SLOTS
AT_EARLY, AT_LATE, AT_FIRST, AT_SECOND = 0, 10, 16, 24
EXTRA = 16
TILE = 64
ROWS = 32
MIB = 1024 * 1024


BF = jnp.bfloat16
F32 = jnp.float32


def sign_of(core):
    return 1 - 2 * core


def dp_perm(kind):
    pairs = []
    for z in range(N_Z):
        for y in range(N_Y):
            for core in range(N_CORE):
                tz, ty, tc = z, y, core
                if kind == "a":
                    tz = (z + sign_of(core)) % N_Z
                elif kind == "b":
                    tz = (z - sign_of(core)) % N_Z
                elif kind == "y":
                    ty = 1 - y
                elif kind == "c":
                    tc = 1 - core
                elif kind == "z1":
                    tz = z ^ 1
                elif kind == "z2":
                    tz = z ^ 2
                elif kind == "z3":
                    tz = z ^ 3
                elif kind == "yc":
                    ty, tc = 1 - y, 1 - core
                pairs.append(((z * N_Y + y) * N_CORE + core, (tz * N_Y + ty) * N_CORE + tc))
    return pairs


def tensor_perm(kind):
    pairs = []
    for dp in range(N_DP):
        step = sign_of(dp % N_CORE)
        for x in range(N_X):
            for ylo in range(N_YLO):
                tx, ty = x, ylo
                if kind == "a":
                    tx = (x + step) % N_X
                elif kind == "b":
                    tx = (x - step) % N_X
                elif kind == "y":
                    ty = 1 - ylo
                else:
                    tx = x ^ int(kind)
                pairs.append((dp * N_TENSOR + x * N_YLO + ylo, dp * N_TENSOR + tx * N_YLO + ty))
    return pairs


def over_dp(value, kind):
    return lax.ppermute(value, "dp", dp_perm(kind))


def over_tensor(value, kind):
    return lax.ppermute(value, ("dp", "tensor"), tensor_perm(kind))


def spec(space):
    return pl.BlockSpec(memory_space=space)


def lanes(index, size=BS):
    return pl.ds(pl.multiple_of(index * size, size), size)


def mm(left, right):
    return jnp.dot(left, right, preferred_element_type=F32)


def mm_t(left, right):
    return lax.dot_general(left, right, (((1,), (1,)), ((), ())), preferred_element_type=F32)


def mm_l(left, right):
    return lax.dot_general(left, right, (((0,), (0,)), ((), ())), preferred_element_type=F32)


def fold(value):
    return sum(value[:, k * BS : (k + 1) * BS] for k in range(value.shape[1] // BS))


def norm_kernel(index, weights, h0, h1, h2, h3, grad_out, gain, normed, stats, kept):
    tile, width = normed.shape
    size, rows = 512, 16

    def some_rows(step, carry):
        here = pl.ds(pl.multiple_of(step * rows, rows), rows)
        zero = jnp.zeros((rows, BS), F32)
        squares, moments, cots = zero, [zero] * 4, [zero] * 4
        for at in range(0, width, size):
            cut = slice(at, at + size)
            layers = [h[0, here, cut].astype(F32) for h in (h0, h1, h2, h3)]
            mixed = weights[0] * layers[0]
            for slot in range(1, 4):
                mixed = mixed + weights[slot] * layers[slot]
            kept[here, cut] = mixed
            squares = squares + fold(mixed * mixed)
            cot = grad_out[here, cut].astype(F32)
            for slot in range(4):
                moments[slot] = moments[slot] + fold(mixed * layers[slot])
                cots[slot] = cots[slot] + fold(cot * layers[slot])
        scale = lax.rsqrt(jnp.sum(squares, axis=-1, keepdims=True) / width + EPSILON)
        for at in range(0, width, size):
            cut = slice(at, at + size)
            normed[here, cut] = (kept[here, cut] * scale * gain[:, cut]).astype(BF)
        lane = lax.broadcasted_iota(jnp.int32, (rows, BS), 1)
        found = jnp.where(lane == 0, scale, 0.0)
        for slot in range(4):
            found = jnp.where(lane == 1 + slot, jnp.sum(moments[slot], axis=-1, keepdims=True), found)
            found = jnp.where(lane == 5 + slot, jnp.sum(cots[slot], axis=-1, keepdims=True), found)
        stats[here] = found
        return carry

    lax.fori_loop(0, tile // rows, some_rows, 0)


def norm_call(depth_index, depth_weights, history, grad_out, gain):
    tokens, width = grad_out.shape

    def layer_spec(slot):
        return pl.BlockSpec((1, TILE, width), lambda i, index: (index[slot], i, 0))

    return pl.pallas_call(
        norm_kernel,
        out_shape=(
            jax.ShapeDtypeStruct((tokens, width), BF),
            jax.ShapeDtypeStruct((tokens, BS), F32),
            jax.ShapeDtypeStruct((tokens, width), F32),
        ),
        grid_spec=pltpu.PrefetchScalarGridSpec(
            num_scalar_prefetch=1,
            grid=(tokens // TILE,),
            in_specs=[spec(pltpu.SMEM)]
            + [layer_spec(slot) for slot in range(4)]
            + [
                pl.BlockSpec((TILE, width), lambda i, index: (i, 0)),
                pl.BlockSpec((1, width), lambda i, index: (0, 0)),
            ],
            out_specs=[
                pl.BlockSpec((TILE, width), lambda i, index: (i, 0)),
                pl.BlockSpec((TILE, BS), lambda i, index: (i, 0)),
                pl.BlockSpec((TILE, width), lambda i, index: (i, 0)),
            ],
        ),
        compiler_params=pltpu.CompilerParams(vmem_limit_bytes=24 * MIB),
        cost_estimate=pl.CostEstimate(flops=tokens * width * 30, bytes_accessed=tokens * width * 12, transcendentals=0),
        name="norm",
    )(depth_index, depth_weights, history, history, history, history, grad_out, gain.reshape(1, width))


def join_kernel(gate, up, down, out, sems):
    share = gate.shape[0]
    copies = [
        pltpu.make_async_copy(ref, out.at[pl.ds(k * share, share)], sems.at[k])
        for k, ref in enumerate((gate, up, down))
    ]
    for copy in copies:
        copy.start()
    for copy in copies:
        copy.wait()


def join_call(gate, up, down):
    return pl.pallas_call(
        join_kernel,
        out_shape=jax.ShapeDtypeStruct((3 * gate.shape[0], BS, BS), BF),
        in_specs=[spec(pl.ANY)] * 3,
        out_specs=spec(pltpu.VMEM),
        scratch_shapes=[pltpu.SemaphoreType.DMA((3,))],
        name="join",
    )(gate, up, down)


def part_copies(shard, held, sems, share, parts, slot):
    here = pl.ds(slot * share, share)
    return [
        pltpu.make_async_copy(
            shard.at[pl.ds(part * share, share)], held.at[here, :, pl.ds(k * BS, BS)], sems.at[slot, k]
        )
        for k, part in enumerate(parts)
    ]


def start_parts(shards, held, sems, share, parts):
    for slot, shard in enumerate(shards):
        for copy in part_copies(shard, held, sems, share, parts, slot):
            copy.start()


def wait_parts(shards, held, sems, share, parts, slot):
    for copy in part_copies(shards[0], held, sems, share, parts, slot):
        copy.wait()


def shard_copies(shard, held_pair, held_down, sems, slot, share):
    here = pl.ds(slot * share, share)
    return [
        pltpu.make_async_copy(shard.at[pl.ds(0, share)], held_pair.at[here, :, pl.ds(0, BS)], sems.at[slot, 0]),
        pltpu.make_async_copy(shard.at[pl.ds(share, share)], held_pair.at[here, :, pl.ds(BS, BS)], sems.at[slot, 1]),
        pltpu.make_async_copy(shard.at[pl.ds(2 * share, share)], held_down.at[here], sems.at[slot, 2]),
    ]


def start_shards(shards, held_pair, held_down, sems, share):
    for slot, shard in enumerate(shards):
        for copy in shard_copies(shard, held_pair, held_down, sems, slot, share):
            copy.start()


def accumulate(share, at, table, rows, cols, normed, grad_out, shards, held_pair, held_down, sems, gate_up, back):
    def one_slot(slot, carry):
        for copy in shard_copies(shards[0], held_pair, held_down, sems, slot, share):
            copy.wait()
        base = table[at + slot] * share
        for j in range(share):
            row, col = rows[base + j], cols[base + j]
            gate_up[col] += mm(normed[:, lanes(row)], held_pair[slot * share + j])
            back[col] += mm_t(grad_out[:, lanes(row)], held_down[slot * share + j])
        return carry

    lax.fori_loop(0, len(shards), one_slot, 0)


def weight_grads(share, at, table, rows, cols, normed, grad_out, hidden, pre, grads, mine, other, sems):
    def stores(chip):
        return [
            pltpu.make_async_copy(grads.at[chip, 0], mine.at[chip], sems.at[chip, 0]),
            pltpu.make_async_copy(grads.at[chip, 1], other.at[chip], sems.at[chip, 1]),
        ]

    def one_chip(chip, carry):
        for flip in range(2):
            base = table[at + chip * 2 + flip] * share
            for j in range(share):
                row, col = rows[base + j], cols[base + j]
                both = mm_l(normed[:, lanes(row)], pre[col]).astype(BF)
                grads[chip, flip, j] = both[:, 0:BS]
                grads[chip, flip, share + j] = both[:, BS:]
                grads[chip, flip, 2 * share + j] = mm_l(hidden[col], grad_out[:, lanes(row)]).astype(BF)
            stores(chip)[flip].start()
        return carry

    lax.fori_loop(0, mine.shape[0], one_chip, 0)
    for chip in range(mine.shape[0]):
        for copy in stores(chip):
            copy.wait()


def early_kernel(share, count, *refs):
    table, rows, cols, normed, grad_out = refs[:5]
    shards = refs[5 : 5 + count]
    gate_up, back = refs[5 + count : 7 + count]
    held_pair, held_down, sems = refs[7 + count :]
    start_shards(shards, held_pair, held_down, sems, share)
    gate_up[...] = jnp.zeros_like(gate_up)
    back[...] = jnp.zeros_like(back)
    accumulate(
        share, AT_EARLY, table, rows, cols, normed, grad_out, shards, held_pair, held_down, sems, gate_up, back
    )


def early_call(table, rows, cols, normed, grad_out, shards, share, col_blocks):
    tokens = normed.shape[0]
    count = len(shards)
    return pl.pallas_call(
        functools.partial(early_kernel, share, count),
        out_shape=(
            jax.ShapeDtypeStruct((col_blocks, tokens, 2 * BS), F32),
            jax.ShapeDtypeStruct((col_blocks, tokens, BS), F32),
        ),
        in_specs=[spec(pltpu.SMEM)] * 3 + [spec(pltpu.VMEM)] * 2 + [spec(pl.ANY)] * count,
        out_specs=(spec(pltpu.VMEM), spec(pltpu.VMEM)),
        scratch_shapes=[
            pltpu.VMEM((count * share, BS, 2 * BS), BF),
            pltpu.VMEM((count * share, BS, BS), BF),
            pltpu.SemaphoreType.DMA((count, 3)),
        ],
        compiler_params=pltpu.CompilerParams(vmem_limit_bytes=18 * MIB),
        cost_estimate=pl.CostEstimate(flops=3 * 56 * 192 * 128 * 256, bytes_accessed=12_000_000, transcendentals=0),
        name="early",
    )(table, rows, cols, normed, grad_out, *shards)


def late_kernel(share, count, *refs):
    table, rows, cols, normed, grad_out, gate_up_in, back_in = refs[:7]
    shards = refs[7 : 7 + count]
    hidden, pre, mine, other = refs[7 + count : 11 + count]
    held_pair, held_down, gate_up, back, grads, sems, store_sems = refs[11 + count :]
    start_shards(shards, held_pair, held_down, sems, share)
    gate_up[...] = gate_up_in[...]
    back[...] = back_in[...]
    accumulate(
        share, AT_LATE, table, rows, cols, normed, grad_out, shards, held_pair, held_down, sems, gate_up, back
    )

    def activate(col, carry):
        gate = gate_up[col, :, 0:BS]
        up = gate_up[col, :, BS:]
        cot = back[col]
        sig = 1.0 / (1.0 + jnp.exp(-gate))
        act = gate * sig
        hidden[col] = (act * up).astype(BF)
        pre[col, :, 0:BS] = (cot * up * sig * (1.0 + gate * (1.0 - sig))).astype(BF)
        pre[col, :, BS:] = (cot * act).astype(BF)
        return carry

    lax.fori_loop(0, hidden.shape[0], activate, 0)
    weight_grads(
        share, AT_FIRST, table, rows, cols, normed, grad_out, hidden, pre, grads, mine, other, store_sems
    )


def late_call(table, rows, cols, normed, grad_out, gate_up, back, shards, share):
    col_blocks, tokens, _ = gate_up.shape
    count = len(shards)
    half = CHIPS // 2
    grads = jax.ShapeDtypeStruct((half, 3 * share, BS, BS), BF)
    return pl.pallas_call(
        functools.partial(late_kernel, share, count),
        out_shape=(
            jax.ShapeDtypeStruct((col_blocks, tokens, BS), BF),
            jax.ShapeDtypeStruct((col_blocks, tokens, 2 * BS), BF),
            grads,
            grads,
        ),
        in_specs=[spec(pltpu.SMEM)] * 3 + [spec(pltpu.VMEM)] * 4 + [spec(pl.ANY)] * count,
        out_specs=(spec(pltpu.VMEM), spec(pltpu.VMEM), spec(pl.ANY), spec(pl.ANY)),
        scratch_shapes=[
            pltpu.VMEM((count * share, BS, 2 * BS), BF),
            pltpu.VMEM((count * share, BS, BS), BF),
            pltpu.VMEM((col_blocks, tokens, 2 * BS), F32),
            pltpu.VMEM((col_blocks, tokens, BS), F32),
            pltpu.VMEM((half, 2, 3 * share, BS, BS), BF),
            pltpu.SemaphoreType.DMA((count, 3)),
            pltpu.SemaphoreType.DMA((half, 2)),
        ],
        compiler_params=pltpu.CompilerParams(vmem_limit_bytes=34 * MIB),
        cost_estimate=pl.CostEstimate(flops=6 * 56 * 192 * 128 * 256, bytes_accessed=20_000_000, transcendentals=0),
        name="late",
    )(table, rows, cols, normed, grad_out, gate_up, back, *shards)


def rest_kernel(share, table, rows, cols, normed, grad_out, hidden, pre, mine, other, grads, store_sems):
    weight_grads(
        share, AT_SECOND, table, rows, cols, normed, grad_out, hidden, pre, grads, mine, other, store_sems
    )


def rest_call(table, rows, cols, normed, grad_out, hidden, pre, share):
    half = CHIPS // 2
    grads = jax.ShapeDtypeStruct((half, 3 * share, BS, BS), BF)
    return pl.pallas_call(
        functools.partial(rest_kernel, share),
        out_shape=(grads, grads),
        in_specs=[spec(pltpu.SMEM)] * 3 + [spec(pltpu.VMEM)] * 4,
        out_specs=(spec(pl.ANY), spec(pl.ANY)),
        scratch_shapes=[
            pltpu.VMEM((half, 2, 3 * share, BS, BS), BF),
            pltpu.SemaphoreType.DMA((half, 2)),
        ],
        compiler_params=pltpu.CompilerParams(vmem_limit_bytes=16 * MIB),
        cost_estimate=pl.CostEstimate(flops=3 * 56 * 192 * 128 * 256, bytes_accessed=10_000_000, transcendentals=0),
        name="rest",
    )(table, rows, cols, normed, grad_out, hidden, pre)


def input_kernel(share, *refs):
    order, rows, cols, place, index, weights, pre, stats, gain = refs[:9]
    history = refs[9]
    shards = refs[10 : 10 + N_DP]
    pieces = refs[10 + N_DP : 14 + N_DP]
    small = refs[14 + N_DP]
    held, layers, total, s_wide, load_sems, layer_sems = refs[15 + N_DP :]
    tokens, width = total.shape
    start_parts(shards, held, load_sems, share, (0, 1))
    layer_copies = [
        pltpu.make_async_copy(history.at[index[slot]], layers.at[slot], layer_sems.at[slot]) for slot in range(4)
    ]
    for copy in layer_copies:
        copy.start()
    total[...] = jnp.zeros_like(total)

    def back_input(slot, carry):
        wait_parts(shards, held, load_sems, share, (0, 1), slot)
        base = order[slot] * share
        for j in range(share):
            row, col = rows[base + j], cols[base + j]
            total[:, lanes(row)] += mm_t(pre[col], held[slot * share + j])
        return carry

    lax.fori_loop(0, N_DP, back_input, 0)
    for copy in layer_copies:
        copy.wait()

    step = sign_of(place[0])
    offsets = (0, step, -step, 2)
    per_part = pieces[0].shape[2] // BS
    small[...] = jnp.zeros_like(small)
    lane = lax.broadcasted_iota(jnp.int32, (1, BS), 1)

    def finish(chunk, carry):
        here = pl.ds(pl.multiple_of(chunk * ROWS, ROWS), ROWS)
        stat = stats[here]
        scale = stat[:, 0:1]
        zero = jnp.zeros((ROWS, BS), F32)
        sums = [zero] * 4
        for way, piece in enumerate(pieces):
            x_there = (place[1] + offsets[way] + 2 * N_X) % N_X
            for part in range(N_YLO):
                half = (part + place[2]) % N_YLO
                for block in range(per_part):
                    row = (x_there * N_YLO + half) * per_part + block
                    where = lanes(row)
                    value = total[here, where]
                    piece[part, here, block * BS : (block + 1) * BS] = value.astype(BF)
                    scaled = value * gain[:, where]
                    mixed = zero
                    for slot in range(4):
                        layer = layers[slot, here, where].astype(F32)
                        sums[slot] = sums[slot] + scaled * layer
                        mixed = mixed + weights[slot] * layer
                    small[pl.ds(row, 1), :] += jnp.sum(value * mixed * scale, axis=0, keepdims=True)
        alphas = [jnp.sum(total_sum, axis=1, keepdims=True) for total_sum in sums]
        s_col = sum(weights[slot] * alphas[slot] for slot in range(4))
        s_wide[here] = jnp.broadcast_to(s_col, (ROWS, BS))
        depth = jnp.zeros((1, BS), F32)
        for slot in range(4):
            per_token = (
                scale * alphas[slot]
                - scale * scale * scale * stat[:, 1 + slot : 2 + slot] * s_col / width
                + stat[:, 5 + slot : 6 + slot] / N_TENSOR
            )
            depth = jnp.where(lane == slot, jnp.sum(per_token, axis=0, keepdims=True), depth)
        small[width // BS : width // BS + 1, :] += depth
        return carry

    lax.fori_loop(0, tokens // ROWS, finish, 0)
    s_row = jnp.transpose(s_wide[...])[0:1]
    for piece in pieces:
        for part in range(N_YLO):
            piece[part, tokens:] = jnp.zeros((EXTRA, piece.shape[2]), BF)
            for block in range(2):
                size = min(BS, tokens - block * BS)
                lead = jnp.broadcast_to(s_row[:, block * BS : block * BS + size], (EXTRA, size))
                piece[part, tokens:, block * BS : block * BS + size] = lead.astype(BF)


def input_call(order, rows, cols, place, depth_index, depth_weights, pre, stats, gain, history, shards, share):
    tokens = pre.shape[1]
    width = history.shape[2]
    piece = jax.ShapeDtypeStruct((N_YLO, tokens + EXTRA, width // N_TENSOR), BF)
    return pl.pallas_call(
        functools.partial(input_kernel, share),
        out_shape=(piece,) * N_X + (jax.ShapeDtypeStruct((width // BS + 8, BS), F32),),
        in_specs=[spec(pltpu.SMEM)] * 6 + [spec(pltpu.VMEM)] * 3 + [spec(pl.ANY)] * (N_DP + 1),
        out_specs=(spec(pltpu.VMEM),) * (N_X + 1),
        scratch_shapes=[
            pltpu.VMEM((N_DP * share, BS, 2 * BS), BF),
            pltpu.VMEM((4, tokens, width), BF),
            pltpu.VMEM((tokens, width), F32),
            pltpu.VMEM((tokens, BS), F32),
            pltpu.SemaphoreType.DMA((N_DP, 2)),
            pltpu.SemaphoreType.DMA((4,)),
        ],
        compiler_params=pltpu.CompilerParams(vmem_limit_bytes=30 * MIB),
        cost_estimate=pl.CostEstimate(flops=2 * 112 * 192 * 128 * 256, bytes_accessed=20_000_000, transcendentals=0),
        name="input_grad",
    )(order, rows, cols, place, depth_index, depth_weights, pre, stats, gain.reshape(1, width), history, *shards)


def output_kernel(share, *refs):
    order, rows, cols, place, hidden = refs[:5]
    shards = refs[5 : 5 + N_DP]
    pieces = refs[5 + N_DP : 9 + N_DP]
    held, total, load_sems = refs[9 + N_DP :]
    start_parts(shards, held, load_sems, share, (2,))
    total[...] = jnp.zeros_like(total)

    def forward(slot, carry):
        wait_parts(shards, held, load_sems, share, (2,), slot)
        base = order[slot] * share
        for j in range(share):
            row, col = rows[base + j], cols[base + j]
            total[:, lanes(row)] += mm(hidden[col], held[slot * share + j])
        return carry

    lax.fori_loop(0, N_DP, forward, 0)
    step = sign_of(place[0])
    offsets = (0, step, -step, 2)
    for way, piece in enumerate(pieces):
        x_there = (place[1] + offsets[way] + 2 * N_X) % N_X
        for part in range(N_YLO):
            half = (part + place[2]) % N_YLO
            size = piece.shape[2]
            piece[part] = total[:, lanes(x_there * N_YLO + half, size)].astype(BF)


def output_call(order, rows, cols, place, hidden, shards, share, width):
    tokens = hidden.shape[1]
    piece = jax.ShapeDtypeStruct((N_YLO, tokens, width // N_TENSOR), BF)
    return pl.pallas_call(
        functools.partial(output_kernel, share),
        out_shape=(piece,) * N_X,
        in_specs=[spec(pltpu.SMEM)] * 4 + [spec(pltpu.VMEM)] + [spec(pl.ANY)] * N_DP,
        out_specs=(spec(pltpu.VMEM),) * N_X,
        scratch_shapes=[
            pltpu.VMEM((N_DP * share, BS, BS), BF),
            pltpu.VMEM((tokens, width), F32),
            pltpu.SemaphoreType.DMA((N_DP, 1)),
        ],
        compiler_params=pltpu.CompilerParams(vmem_limit_bytes=16 * MIB),
        cost_estimate=pl.CostEstimate(flops=112 * 192 * 128 * 256, bytes_accessed=10_000_000, transcendentals=0),
        name="output",
    )(order, rows, cols, place, hidden, *shards)


def barrier(*values):
    return lax.optimization_barrier(values)


def add(*values):
    return sum(v.astype(F32) for v in values)


def reduce_tensor(pieces, after, last, first=None):
    own, to_a, to_b, far = pieces
    from_far = over_tensor(far, "a")
    if first is not None:
        from_far, _ = barrier(from_far, first)
    near = add(to_a, from_far).astype(BF)
    from_a, _ = barrier(over_tensor(near, "a"), after)
    total = add(own, from_a, over_tensor(to_b, "b"))
    moved, _ = barrier(over_tensor(total[1].astype(BF), "y"), last)
    return add(total[0], moved)


def reduce_small(small, after):
    small = small + over_dp(small, "c")
    small = small + over_dp(small, "y")
    moved, _ = barrier(over_tensor(small, "y"), after)
    small = small + moved
    one, two, three = [over_dp(small, kind) for kind in ("z1", "z2", "z3")]
    small = (small + one) + (two + three)
    one, two, three = [over_tensor(small, kind) for kind in ("1", "2", "3")]
    return (small + one) + (two + three)


def per_device(
    history,
    depth_weights,
    depth_index,
    gain,
    gate_blocks,
    up_blocks,
    down_blocks,
    block_ids,
    grad_out,
):
    tokens, width = grad_out.shape
    share = gate_blocks.shape[0]
    col_blocks = 14
    share_width = width // N_TENSOR
    dp = lax.axis_index("dp")
    tensor = lax.axis_index("tensor")
    core = dp % N_CORE
    share_start = tensor * share_width

    ahead = jnp.array([AHEAD[chip] for chip, _ in TABLE], jnp.int32)
    turn = jnp.array([TURN[chip] for chip, _ in TABLE], jnp.int32)
    flip = jnp.array([f for _, f in TABLE], jnp.int32)
    there = (core + flip) % N_CORE
    table = (
        ((dp // (N_Y * N_CORE) + ahead * sign_of(there) + 2 * N_Z) % N_Z) * (N_Y * N_CORE)
        + ((dp // N_CORE + turn) % N_Y) * N_CORE
        + there
    ).astype(jnp.int32)
    rows, cols = block_ids[:, 0], block_ids[:, 1]
    where = jnp.arange(4, dtype=jnp.int32)
    place = jnp.where(where == 0, core, jnp.where(where == 1, tensor // N_YLO, tensor % N_YLO)).astype(jnp.int32)

    got = {}
    own = join_call(gate_blocks, up_blocks, down_blocks)
    got[OWN, 0] = own
    got[A1, 0] = over_dp(own, "a")
    got[B1, 0] = over_dp(own, "b")
    got[YY, 0] = over_dp(own, "y")
    normed, stats, kept = norm_call(depth_index, depth_weights, history, grad_out, gain)
    got[A2, 0] = over_dp(got[A1, 0], "a")
    got[YA, 0] = over_dp(got[YY, 0], "a")
    got[YB, 0] = over_dp(got[YY, 0], "b")
    got[Y2, 0] = over_dp(got[A2, 0], "y")
    for chip in range(CHIPS):
        got[chip, 1] = over_dp(got[chip, 0], "c")

    gate_up, back = early_call(
        table, rows, cols, normed, grad_out, [got[key] for key in EARLY], share, col_blocks
    )
    hidden, pre, mine1, other1 = late_call(
        table, rows, cols, normed, grad_out, gate_up, back, [got[key] for key in LATE], share
    )
    arrived1 = over_dp(other1, "c")
    mine2, other2 = rest_call(table, rows, cols, normed, grad_out, hidden, pre, share)
    arrived2 = over_dp(other2, "c")
    part = {}
    for k in range(CHIPS // 2):
        part[SECOND[k]] = add(mine2[k], arrived2[k])
    far_y = over_dp(add(mine1[0], arrived1[0]).astype(BF), "y")
    across_a = over_dp(add(mine1[1], arrived1[1]).astype(BF), "a")
    both_b = over_dp(add(mine1[2:4], arrived1[2:4]).astype(BF), "b")

    shards = [got[key] for key in EARLY + LATE]
    *back_pieces, small = input_call(
        table, rows, cols, place, depth_index, depth_weights, pre, stats, gain, history, shards, share
    )
    out_pieces = output_call(table, rows, cols, place, hidden, shards, share, width)

    near_b = both_b[1]
    mine_y, arrived_y, across_a, across_b = barrier(mine2, arrived2, across_a, both_b)
    across_b = across_b[0]
    at = SECOND.index(YY)
    part[YY] = add(mine_y[at], arrived_y[at])
    far = add(part[A2], far_y).astype(BF)
    near = add(part[B1], over_dp(far, "a")).astype(BF)
    across_low = add(part[YY], across_a, across_b).astype(BF)
    across = over_dp(across_low, "y")
    near_a = over_dp(near, "a")
    own1, own2 = mine2[SECOND.index(OWN)], arrived2[SECOND.index(OWN)]
    block_grads = [
        add(*[v[k * share : (k + 1) * share] for v in (own1, own2, near_a, near_b, across)]) for k in range(3)
    ]

    back = reduce_tensor(back_pieces, near, block_grads[0], across_low)
    ffn = reduce_tensor(out_pieces, near, block_grads[0])
    small = reduce_small(small, across_low)

    mixed = lax.dynamic_slice_in_dim(kept, share_start, share_width, 1)
    layer_out = (mixed + ffn).astype(BF)

    scale = stats[:, 0:1]
    gain_share = lax.dynamic_slice_in_dim(gain, share_start, share_width, 0)
    cot = lax.dynamic_slice_in_dim(grad_out, share_start, share_width, 1).astype(F32)
    s_col = back[tokens, 0:tokens].reshape(tokens, 1)
    grad_mixed = cot + scale * gain_share * back[0:tokens] - mixed * (scale * scale * scale) * (s_col / width)

    return (
        layer_out,
        grad_mixed,
        block_grads[0],
        block_grads[1],
        block_grads[2],
        small[width // BS, 0:4],
        lax.dynamic_slice_in_dim(small, share_start // BS, share_width // BS, 0).reshape(share_width),
    )


def solution(mesh):
    placed = (
        P(None, "dp", None),
        P(),
        P(),
        P(),
        P(("tensor", "dp"), None, None),
        P(("tensor", "dp"), None, None),
        P(("tensor", "dp"), None, None),
        P("tensor", None),
        P("dp", None),
    )

    return jax.shard_map(
        per_device,
        mesh=mesh,
        in_specs=placed,
        out_specs=(
            P("dp", "tensor"),
            P("dp", "tensor"),
            P(("tensor", "dp"), None, None),
            P(("tensor", "dp"), None, None),
            P(("tensor", "dp"), None, None),
            P(),
            P("tensor"),
        ),
        check_vma=False,
    )
```
